32 devices in a mesh: group: 4 (over x, core), replica: 8 (over z, y).
Axes of the slice: x: 2, y: 2, z: 4, core: 2. Of those that a mesh axis runs over, the one named last changes fastest.
Arguments:
- tokens: bfloat16 [16, 1024, 384], P('replica', 'group'), may hold values from -6 to 6
- cotangent: bfloat16 [16, 1024, 384], P('replica', 'group'), may hold values from -6 to 6
- weight: float32 [1774592], P('group'), may hold values from -1.6329932 to 1.6329932
- momentum: float32 [1774592], P('group'), may hold values from -40 to 40
- average: float32 [1774592], P('group'), may hold values from -1.6329932 to 1.6329932
- rate: float32 [1], replicated, may hold values from 0.00015625 to 0.000625
- step: int32 [1], replicated, may hold values from 1 to 20
Outputs:
- output: bfloat16 [16, 1024, 384], P('replica', 'group')
- grad_tokens: bfloat16 [16, 1024, 384], P('replica', 'group')
- grad: float32 [1774592], P('group')
- momentum_new: float32 [1774592], P('group')
- average_new: float32 [1774592], P('group')
- weight_new: float32 [1774592], P('group')
- weight_copy: bfloat16 [1774592], P('group')
The draws below stay inside these ranges and needn't reach their ends.
All inputs are finite; a program needn't handle non-finite values.
Results may differ from the reference program's by a relative error of at most 0.013.
The reference program's roundings to bfloat16 on the way count: a program that leaves them out, or rounds other values in their place, can miss the bound.
Values may be sent and summed in bfloat16 or wider, within the bound.
No kernel may reach another device: no remote copies, remote signals or barrier semaphores. Data moves between devices by JAX's collectives and lax.ppermute only.
A program may use at most 448 MiB of HBM per device.

```python
import math
import jax
import jax.numpy as jnp
from jax import lax

D = 384
H = 6
DH = 64
FF = 1536
PATCHES = 1024
IMAGES = 16
TOKENS = 16384
P_SIZE = 1774592


def param_law(key):
    layout = ((D * 3 * D, D ** (-0.5), 0.0, 0.0), (D * D, 8.0 * D ** (-0.5), 0.0, 0.0), (D * FF, D ** (-0.5), 0.0, 0.0), (FF * D, FF ** (-0.5), 0.0, 0.0), (D, 0.0, 0.2, 1.0), (D, 0.2, 0.0, 0.0), (3 * D, 0.2, 0.0, 0.0), (DH, 0.0, 0.2, 1.2), (DH, 0.0, 0.2, 1.2), (D, 0.2, 0.0, 0.0), (D, 0.0, 0.2, 1.0), (D, 0.2, 0.0, 0.0), (FF, 0.2, 0.0, 0.0), (D, 0.2, 0.0, 0.0))
    normal_part = jnp.clip(jax.random.normal(jax.random.fold_in(key, 11), (P_SIZE,), jnp.float32), -4.0, 4.0)
    uniform_part = jax.random.uniform(jax.random.fold_in(key, 12), (P_SIZE,), jnp.float32, -1.0, 1.0)
    normal_scale = jnp.concatenate([jnp.full((seg_len,), spread, jnp.float32) for seg_len, spread, wobble, center in layout])
    uniform_scale = jnp.concatenate([jnp.full((seg_len,), wobble, jnp.float32) for seg_len, spread, wobble, center in layout])
    centers = jnp.concatenate([jnp.full((seg_len,), center, jnp.float32) for seg_len, spread, wobble, center in layout])
    return centers + normal_scale * normal_part + uniform_scale * uniform_part


def draw_weight(key, part):
    return param_law(jax.random.fold_in(key, 1))


def draw_average(key, part):
    return param_law(jax.random.fold_in(key, 2))


def level_of(stream_key, shape, cuts, smallest, largest):
    loudness, own = 1.0, jax.random.fold_in(stream_key, 6)
    for dim, parts in cuts:
        heights = jnp.exp(jax.random.uniform(jax.random.fold_in(own, dim), (parts,), jnp.float32, smallest / len(cuts), largest / len(cuts)))
        loudness = loudness * jnp.repeat(heights, shape[dim] // parts).reshape([-1 if axis == dim else 1 for axis in range(len(shape))])
    return loudness


def gaussian(own_key, shape, scale, limit, cuts=(), dtype=jnp.bfloat16):
    factor_of = level_of(own_key, shape, cuts, -0.22, 0.18) if cuts else 1.0
    values = jax.random.normal(own_key, shape, jnp.float32) * scale * factor_of
    return jnp.minimum(jnp.maximum(values, -limit), limit).astype(dtype)


def setup_inputs(seed: int = 0) -> dict:
    streams_of = jax.random.split(jax.random.key(seed), 8)
    return {
        "tokens": gaussian(streams_of[0], (IMAGES, PATCHES, D), 1.0, 6.0, ((0, 8), (1, 4))),
        "cotangent": gaussian(streams_of[1], (IMAGES, PATCHES, D), 1.0, 6.0, ((0, 8), (1, 4))),
        "weight": draw_weight(jax.random.fold_in(streams_of[7], 71), 0),
        "momentum": gaussian(streams_of[3], (P_SIZE,), (0.05 * TOKENS ** 0.5), 40.0, ((0, 4),), jnp.float32),
        "average": draw_average(jax.random.fold_in(streams_of[7], 71), 0),
        "rate": jnp.clip(jnp.exp(jax.random.uniform(streams_of[5], (1,), jnp.float32, math.log(0.00015625), math.log(0.000625))), 0.00015625, 0.000625),
        "step": jax.random.randint(streams_of[6], (1,), 1, 21).astype(jnp.int32),
    }


EPSILON = 1e-06
MOMENT = 0.9
DECAY_MAX = 0.999
HIGH = lax.Precision.HIGHEST

@jax.custom_vjp
def low(v):
    return lax.optimization_barrier(v.astype(jnp.bfloat16)).astype(jnp.float32)

@jax.custom_vjp
def low_back(v):
    return v

def low_keep(v):
    return (low(v), None)

def low_pass(kept, grad):
    return (grad,)

def back_keep(v):
    return (v, None)

def back_low(kept, grad):
    return (low(grad),)
low.defvjp(low_keep, low_pass)
low_back.defvjp(back_keep, back_low)

def split_params(flat_vec):
    layout = ((D * 3 * D, (D, 3 * D)), (D * D, (D, D)), (D * FF, (D, FF)), (FF * D, (FF, D)), (D, (D,)), (D, (D,)), (3 * D, (3 * D,)), (DH, (DH,)), (DH, (DH,)), (D, (D,)), (D, (D,)), (D, (D,)), (FF, (FF,)), (D, (D,)))
    pieces = []
    offset = 0
    for seg_len, seg_shape in layout:
        pieces.append(flat_vec[offset:offset + seg_len].reshape(seg_shape))
        offset = offset + seg_len
    return tuple(pieces)

def layer_norm(values, scale, shift):
    center = values - lax.optimization_barrier(jnp.mean(values, -1, keepdims=True))
    spread = lax.optimization_barrier(jnp.mean(center * center, -1, keepdims=True))
    return center * lax.rsqrt(spread + EPSILON) * scale + shift

def matmul(left, right):
    return jnp.einsum('gtd,de->gte', left, right, precision=HIGH)

def forward(images_in, flat_vec):
    params = low(flat_vec)
    w_qkv, w_out, w_fc1, w_fc2, gain_one, bias_one, bias_qkv, gain_query, gain_key, bias_out, gain_two, bias_two, bias_fc1, bias_fc2 = split_params(params)
    group_len = images_in.shape[0]
    act_one = low(layer_norm(images_in, gain_one, bias_one))
    qkv_all = low_back(matmul(act_one, w_qkv) + bias_qkv)
    head_shape = (group_len, PATCHES, H, DH)
    query = qkv_all[..., :D].reshape(head_shape)
    key_val = qkv_all[..., D:2 * D].reshape(head_shape)
    value = qkv_all[..., 2 * D:].reshape(head_shape)
    query = low(low_back(layer_norm(query, gain_query, 0.0)))
    key_val = low(low_back(layer_norm(key_val, gain_key, 0.0)))
    value = low(low_back(value))
    scores = low_back(jnp.einsum('gqhd,gkhd->ghqk', query, key_val, precision=HIGH) * DH ** (-0.5))
    probs = low(jax.nn.softmax(scores, axis=-1))
    attn = jnp.einsum('ghqk,gkhd->gqhd', probs, value, precision=HIGH).reshape(group_len, PATCHES, D)
    attn = low(low_back(attn))
    resid_mid = images_in + low_back(matmul(attn, w_out) + bias_out)
    act_two = low(layer_norm(resid_mid, gain_two, bias_two))
    hidden_pre = low_back(matmul(act_two, w_fc1) + bias_fc1)
    hidden = low(jax.nn.gelu(hidden_pre, approximate=False))
    return resid_mid + low_back(matmul(hidden, w_fc2) + bias_fc2)

def reference(tokens, cotangent, weight, momentum, average, rate, step):
    block_count = IMAGES // 4
    inputs = tokens.astype(jnp.float32).reshape(block_count, 4, PATCHES, D)
    pulled = cotangent.astype(jnp.float32).reshape(block_count, 4, PATCHES, D)

    def one_block(total, pair_in):
        image_in, image_cot = pair_in
        result, pullback = jax.vjp(forward, image_in, weight)
        grad_in, grad_weight = pullback(image_cot)
        return (total + grad_weight, (result.astype(jnp.bfloat16), grad_in.astype(jnp.bfloat16)))
    grad_sum, (outputs, grad_inputs) = lax.scan(one_block, jnp.zeros(weight.shape, jnp.float32), (inputs, pulled))
    momentum_new = MOMENT * momentum + grad_sum
    weight_new = weight - rate[0] * (grad_sum + MOMENT * momentum_new)
    step_value = step[0].astype(jnp.float32)
    ema_decay = jnp.minimum(DECAY_MAX, (1.0 + step_value) / (10.0 + step_value))
    average_new = ema_decay * average + (1.0 - ema_decay) * weight_new
    return (outputs.reshape(IMAGES, PATCHES, D), grad_inputs.reshape(IMAGES, PATCHES, D), grad_sum, momentum_new, average_new, weight_new, weight_new.astype(jnp.bfloat16))
```

```python
import jax
import jax.numpy as jnp
from jax import lax
from jax.experimental import pallas as pl
from jax.experimental.pallas import tpu as pltpu
from jax.sharding import PartitionSpec as P

D = 384
H = 6
DH = 64
FF = 1536
EPSILON = 1e-06
MOMENT = 0.9
DECAY_MAX = 0.999
INV_ROOT_TWO = 0.7071067811865476
INV_ROOT_TAU = 0.3989422804014327
SCALE = DH ** (-0.5)

ROW_OUT = 3456
ROW_FC1 = 4608
ROW_FC2 = 9216
ROW_VEC = 13824
ROWS = 13864
QUARTER = 3466
PAD_Q = 3488
ROWS_A = ROW_VEC - ROW_OUT
PAD_A = 10496
PAD_B = 3584

F32 = jnp.float32
BF16 = jnp.bfloat16


def dot_nn(a, b):
    return lax.dot_general(a, b, (((1,), (0,)), ((), ())), preferred_element_type=F32)


def dot_nt(a, b):
    return lax.dot_general(a, b, (((1,), (1,)), ((), ())), preferred_element_type=F32)


def dot_tn(a, b):
    return lax.dot_general(a, b, (((0,), (0,)), ((), ())), preferred_element_type=F32)


def row_of(vec, start, count):
    return jnp.concatenate([vec[start + i : start + i + 1] for i in range(count)], axis=1)


def norm(values):
    center = values - jnp.mean(values, -1, keepdims=True)
    inv = lax.rsqrt(jnp.mean(center * center, -1, keepdims=True) + EPSILON)
    return center * inv, inv


def norm_back(grad_norm, normed, inv):
    inner = jnp.mean(grad_norm * normed, -1, keepdims=True)
    return inv * (grad_norm - jnp.mean(grad_norm, -1, keepdims=True) - normed * inner)


def head_mean_matrix():
    r = lax.broadcasted_iota(jnp.int32, (256, 128), 0)
    c = lax.broadcasted_iota(jnp.int32, (256, 128), 1)
    return jnp.where((r % 128) // DH == c // DH, 1.0 / DH, 0.0).astype(BF16)


def head_mean(x, matrix):
    hi = x.astype(BF16)
    lo = (x - hi.astype(F32)).astype(BF16)
    return dot_nn(jnp.concatenate([hi, lo], axis=1), matrix)


def lane_head(rows, h):
    lane = lax.broadcasted_iota(jnp.int32, (rows, 128), 1)
    return (lane // DH) == h, lane - DH * (1 - h)


def qkv_attend_kernel(
    xo_ref, xt_ref, wf_ref, vec_ref,
    act_ref, w2_ref, qx_ref, k_ref, v_ref, out_ref, nq_ref, iq_ref, nk_ref, ik_ref,
    flat, q_s,
):
    rows = xo_ref.shape[0]
    vec = vec_ref[...].astype(F32)
    gain_one, bias_one, bias_qkv = row_of(vec, 0, 3), row_of(vec, 3, 3), row_of(vec, 6, 9)
    gains = vec[15:16]
    gain_q = jnp.concatenate([gains[:, :DH], gains[:, :DH]], axis=1)
    gain_k = jnp.concatenate([gains[:, DH:], gains[:, DH:]], axis=1)
    flat[...] = wf_ref[...].astype(F32)
    for j in range(9):
        w2_ref[:, 128 * j : 128 * j + 128] = flat[pl.ds(j, D, stride=9), :].astype(BF16)
    step = 256

    def ln(ref, base):
        def body(i, c):
            at = pl.multiple_of(i * step, step)
            n, _ = norm(ref[pl.ds(at, step), :].astype(F32))
            act_ref[pl.ds(at + base, step), :] = (n * gain_one + bias_one).astype(BF16)
            return c
        lax.fori_loop(0, rows // step, body, 0)

    ln(xo_ref, 0)
    ln(xt_ref, rows)
    matrix = head_mean_matrix()

    def heads(x, gain, n_ref, i_ref, at, p):
        c = x - head_mean(x, matrix)
        inv = lax.rsqrt(head_mean(c * c, matrix) + EPSILON)
        n = c * inv
        n_ref[pl.ds(at, step), 128 * p : 128 * p + 128] = n
        i_ref[pl.ds(at, step), 128 * p : 128 * p + 128] = inv
        return n * gain

    def project_q(i, c):
        at = pl.multiple_of(i * step, step)
        x = dot_nn(act_ref[pl.ds(at, step), :], w2_ref[:, :D]) + bias_qkv[:, :D]
        for p in range(3):
            y = heads(x[:, 128 * p : 128 * p + 128], gain_q, nq_ref, iq_ref, at, p)
            q_s[p, pl.ds(at, step), :] = y.astype(BF16) * BF16(SCALE)
        return c

    lax.fori_loop(0, rows // step, project_q, 0)

    def project_kv(i, c):
        at = pl.multiple_of(i * step, step)
        x = dot_nn(act_ref[pl.ds(at, step), :], w2_ref[:, D:]) + bias_qkv[:, D:]
        for p in range(3):
            y = heads(x[:, 128 * p : 128 * p + 128], gain_k, nk_ref, ik_ref, at, p)
            k_ref[p, pl.ds(at, step), :] = y.astype(BF16)
            v_ref[p, pl.ds(at, step), :] = x[:, D + 128 * p : D + 128 * p + 128].astype(BF16)
        return c

    lax.fori_loop(0, 2 * rows // step, project_kv, 0)

    def attend(p, c):
        q, k, v = q_s[p], k_ref[p], v_ref[p]
        parts = []
        for h in range(2):
            mine, _ = lane_head(2 * rows, h)
            own, other = lane_head(rows, h)
            qm = jnp.where(own, q, BF16(0.0))
            e = jnp.exp(dot_nt(qm, k)).astype(BF16)
            o = dot_nn(e, jnp.where(mine, v, BF16(1.0)))
            total = pltpu.roll(o, DH, 1)
            parts.append(o / total)
            neg = -jnp.log(o)
            hi = neg.astype(BF16)
            mid_f = neg - hi.astype(F32)
            mid = mid_f.astype(BF16)
            low = (mid_f - mid.astype(F32)).astype(BF16)
            spare = jnp.where(other == 0, hi, jnp.where(other == 1, mid, jnp.where(other == 2, low, BF16(0.0))))
            qx_ref[2 * p + h] = jnp.where(own, qm, spare)
        own, _ = lane_head(rows, 0)
        out_ref[p] = jnp.where(own, parts[0], parts[1])
        return c

    lax.fori_loop(0, 3, attend, 0)


def mlp_kernel(
    x_ref, o_ref, cot_ref, q0_ref, q1_ref, q2_ref, q3_ref,
    out_ref, gmid_ref, gattn_ref, da_ref, dv_ref,
    flat, wo_s, w1_s, w2_s, act_s, n_s, mid_s, gn_s, y_s, db1_s,
):
    rows = x_ref.shape[0]
    flat[0:10, :] = q0_ref[ROW_OUT : ROW_OUT + 10, :].astype(F32)
    flat[10 : 10 + QUARTER, :] = q1_ref[0:QUARTER, :].astype(F32)
    flat[10 + QUARTER : 10 + 2 * QUARTER, :] = q2_ref[0:QUARTER, :].astype(F32)
    flat[10 + 2 * QUARTER : 10 + 3 * QUARTER, :] = q3_ref[0:QUARTER, :].astype(F32)
    vec = flat[ROWS_A : ROWS_A + 40, :]
    bias_out, gain_two, bias_two = row_of(vec, 16, 3), row_of(vec, 19, 3), row_of(vec, 22, 3)
    bias_fc1, bias_fc2 = row_of(vec, 25, 12), row_of(vec, 37, 3)
    for j in range(3):
        wo_s[:, 128 * j : 128 * j + 128] = flat[pl.ds(j, D, stride=3), :].astype(BF16)
        w2_s[:, 128 * j : 128 * j + 128] = flat[pl.ds(ROW_FC2 - ROW_OUT + j, FF, stride=3), :].astype(BF16)
    for j in range(12):
        w1_s[:, 128 * j : 128 * j + 128] = flat[pl.ds(ROW_FC1 - ROW_OUT + j, D, stride=12), :].astype(BF16)

    attn = jnp.concatenate([o_ref[p].astype(BF16) for p in range(3)], axis=1)
    mid = x_ref[...].astype(F32) + dot_nn(attn, wo_s[...]) + bias_out
    mid_s[...] = mid
    n, inv = norm(mid)
    n_s[...] = n
    act_s[...] = (n * gain_two + bias_two).astype(BF16)
    y_s[...] = mid + bias_fc2
    gn_s[...] = jnp.zeros_like(gn_s)
    width = 256
    for f in range(FF // width):
        at = f * width
        w1 = w1_s[:, at : at + width]
        w2 = w2_s[at : at + width, :]
        x = dot_nn(act_s[...], w1) + bias_fc1[:, at : at + width]
        phi = 0.5 * (1.0 + lax.erf(x * INV_ROOT_TWO))
        hid = (x * phi).astype(BF16)
        slope = phi + x * jnp.exp(-0.5 * x * x) * INV_ROOT_TAU
        g = dot_nt(cot_ref[...], w2) * slope
        gb = g.astype(BF16)
        y_s[...] += dot_nn(hid, w2)
        gn_s[...] += dot_nt(gb, w1)
        dw2 = dot_tn(hid, cot_ref[...])
        for j in range(3):
            flat[pl.ds(ROW_FC2 - ROW_OUT + 3 * at + j, width, stride=3), :] = dw2[:, 128 * j : 128 * j + 128]
        dw1 = dot_tn(act_s[...], gb)
        for j in range(width // 128):
            flat[pl.ds(ROW_FC1 - ROW_OUT + at // 128 + j, D, stride=12), :] = dw1[:, 128 * j : 128 * j + 128]
        db1_s[:, at : at + width] = jnp.sum(gb.astype(F32), 0, keepdims=True)
    out_ref[...] = y_s[...].astype(BF16)
    gn = gn_s[...]
    cot = cot_ref[...].astype(F32)
    gmid = cot + norm_back(gn * gain_two, n_s[...], inv)
    gmid_ref[...] = gmid
    gproj = gmid.astype(BF16)
    gattn_ref[...] = dot_nt(gproj, wo_s[...]).astype(BF16)
    dwo = dot_tn(attn, gproj)
    for j in range(3):
        flat[pl.ds(j, D, stride=3), :] = dwo[:, 128 * j : 128 * j + 128]
    da_ref[0:ROWS_A, :] = flat[0:ROWS_A, :].astype(BF16)
    da_ref[ROWS_A:, :] = jnp.zeros((PAD_A - ROWS_A, 128), BF16)

    def put(at, row):
        for i in range(row.shape[1] // 128):
            dv_ref[at + i : at + i + 1, :] = row[:, 128 * i : 128 * i + 128]

    put(0, jnp.sum(gproj.astype(F32), 0, keepdims=True))
    put(3, jnp.sum(gn * n_s[...], 0, keepdims=True))
    put(6, jnp.sum(gn, 0, keepdims=True))
    put(9, db1_s[...])
    put(21, jnp.sum(cot, 0, keepdims=True))


def attend_back_kernel(
    xo_ref, xt_ref, act_ref, w2_ref, qx_ref, k_ref, v_ref, out_ref, nq_ref, iq_ref, nk_ref, ik_ref,
    vec_ref, ga_ref, gmid_ref, dv_ref,
    db_ref, go_ref, gt_ref,
    flat, ga_s, gq_s, gk_s, gv_s, gqkv_s, vrow_s,
):
    rows = xo_ref.shape[0]
    vec = vec_ref[...].astype(F32)
    gain_one = row_of(vec, 0, 3)
    gains = vec[15:16]
    gain_q = jnp.concatenate([gains[:, :DH], gains[:, :DH]], axis=1)
    gain_k = jnp.concatenate([gains[:, DH:], gains[:, DH:]], axis=1)
    matrix = head_mean_matrix()
    for p in range(3):
        ga_s[p] = ga_ref[:, 128 * p : 128 * p + 128]

    def back(p, c):
        k, v, ga = k_ref[p], v_ref[p], ga_s[p]
        inner = -float(DH) * head_mean(ga.astype(F32) * out_ref[p], matrix)
        inner = pltpu.roll(inner, DH, 1)
        hi = inner.astype(BF16)
        mid_f = inner - hi.astype(F32)
        mid = mid_f.astype(BF16)
        low = (mid_f - mid.astype(F32)).astype(BF16)
        gq_t = jnp.zeros((128, rows), F32)
        gk = jnp.zeros((2 * rows, 128), F32)
        gv = jnp.zeros((2 * rows, 128), F32)
        for h in range(2):
            mine, other_all = lane_head(2 * rows, h)
            own, other = lane_head(rows, h)
            ones = jnp.where((other_all >= 0) & (other_all <= 2), 1.0, 0.0).astype(BF16)
            qx = qx_ref[2 * p + h]
            spare = jnp.where(other == 0, hi, jnp.where(other == 1, mid, jnp.where(other == 2, low, BF16(0.0))))
            gax = jnp.where(own, ga, spare)
            prob = jnp.exp(dot_nt(jnp.where(mine, k, ones), qx))
            gprob = dot_nt(jnp.where(mine, v, ones), gax)
            gs = (prob * gprob).astype(BF16)
            gv = gv + dot_nn(prob.astype(BF16), jnp.where(own, ga, BF16(0.0)))
            gk = gk + dot_nn(gs, jnp.where(own, qx, BF16(0.0)))
            gq_t = gq_t + dot_tn(jnp.where(mine, k, BF16(0.0)), gs)
        gq_s[p] = (gq_t.T * SCALE).astype(BF16).astype(F32)
        gk_s[p] = gk.astype(BF16).astype(F32)
        gv_s[p] = gv.astype(BF16)
        return c

    lax.fori_loop(0, 3, back, 0)

    def head_back(u, n, inv, gain):
        dn = u * gain
        return inv * (dn - head_mean(dn, matrix) - n * head_mean(dn * n, matrix))

    def put(at, row):
        for i in range(row.shape[1] // 128):
            vrow_s[at + i : at + i + 1, :] = row[:, 128 * i : 128 * i + 128]

    dgq = jnp.zeros((1, 128), F32)
    dgk = jnp.zeros((1, 128), F32)
    for p in range(3):
        sl = slice(128 * p, 128 * p + 128)
        n = nq_ref[:, sl]
        u = gq_s[p]
        dgq = dgq + jnp.sum(u * n, 0, keepdims=True)
        gqkv_s[0:rows, sl] = head_back(u, n, iq_ref[:, sl], gain_q).astype(BF16)
        n = nk_ref[:, sl]
        u = gk_s[p]
        dgk = dgk + jnp.sum(u * n, 0, keepdims=True)
        gqkv_s[:, D + 128 * p : D + 128 * p + 128] = head_back(u, n, ik_ref[:, sl], gain_k).astype(BF16)
        gqkv_s[:, 2 * D + 128 * p : 2 * D + 128 * p + 128] = gv_s[p]
    dgq = dgq + pltpu.roll(dgq, DH, 1)
    dgk = dgk + pltpu.roll(dgk, DH, 1)
    own, _ = lane_head(1, 0)
    put(15, jnp.where(own, dgq, dgk))
    gqkv_q = gqkv_s[0:rows, 0:D]
    gqkv_kv = gqkv_s[:, D:]
    put(6, jnp.sum(gqkv_q.astype(F32), 0, keepdims=True))
    put(9, jnp.sum(gqkv_kv.astype(F32), 0, keepdims=True))
    dwq = dot_tn(act_ref[0:rows, :], gqkv_q)
    dwkv = dot_tn(act_ref[...], gqkv_kv)
    for j in range(3):
        flat[pl.ds(j, D, stride=9), :] = dwq[:, 128 * j : 128 * j + 128]
    for j in range(6):
        flat[pl.ds(3 + j, D, stride=9), :] = dwkv[:, 128 * j : 128 * j + 128]
    db_ref[0:ROW_OUT, :] = flat[...].astype(BF16)
    u_own = dot_nt(gqkv_q, w2_ref[:, 0:D]) + dot_nt(gqkv_kv[0:rows], w2_ref[:, D:])
    u_oth = dot_nt(gqkv_kv[rows:], w2_ref[:, D:])
    n_own, inv_own = norm(xo_ref[...].astype(F32))
    n_oth, inv_oth = norm(xt_ref[...].astype(F32))
    put(0, jnp.sum(u_own * n_own, 0, keepdims=True) + jnp.sum(u_oth * n_oth, 0, keepdims=True))
    put(3, jnp.sum(u_own, 0, keepdims=True) + jnp.sum(u_oth, 0, keepdims=True))
    go_ref[...] = gmid_ref[...] + norm_back(u_own * gain_one, n_own, inv_own)
    gt_ref[...] = norm_back(u_oth * gain_one, n_oth, inv_oth).astype(BF16)
    vrow_s[16:40, :] = dv_ref[...]
    vrow_s[40:128, :] = jnp.zeros((88, 128), F32)
    db_ref[ROW_OUT:, :] = vrow_s[...].astype(BF16)


def shape(*dims, dtype=BF16):
    return jax.ShapeDtypeStruct(dims, dtype)


def vmem(*dims, dtype=BF16):
    return pltpu.VMEM(dims, dtype)


def per_device(tokens, cotangent, weight, momentum, average, rate, step, replicas):
    _, own_len, width = tokens.shape
    rows = 2 * own_len
    place = lax.axis_index("group")
    x, c = place // 2, place % 2
    rep = lax.axis_index("replica")

    def swap(a, bit):
        return lax.ppermute(a, "group", [(i, i ^ bit) for i in range(4)])

    def swap_rep(a, bit):
        return lax.ppermute(a, "replica", [(i, i ^ bit) for i in range(replicas)])

    def pick(a, i):
        return lax.dynamic_index_in_dim(a, i, 0, keepdims=False)

    def across(a):
        return jnp.concatenate([pick(a, x), swap(pick(a, 1 - x), 2)], axis=0)

    xo = across(tokens)
    xt = swap(xo, 1)
    shard = jnp.pad(weight.reshape(QUARTER, 128).astype(BF16), ((0, PAD_Q - QUARTER), (0, 0)))
    beside = swap(shard, 1)
    half = PAD_Q // 2

    def half_of(a):
        return lax.dynamic_slice_in_dim(a, c * half, half, 0)

    def both(mine):
        theirs = swap(mine, 1)
        return jnp.where(c == 0, jnp.concatenate([mine, theirs]), jnp.concatenate([theirs, mine]))

    first = both(swap(half_of(jnp.where(c == x, shard, beside)), 2))
    second = both(swap(half_of(jnp.where(c == x, beside, shard)), 2))
    even = jnp.where(c == 0, shard, beside)
    odd = jnp.where(c == 0, beside, shard)
    q0 = jnp.where(x == 0, even, first)
    q1 = jnp.where(x == 0, odd, second)
    q2 = jnp.where(x == 0, second, even)
    q3 = jnp.where(x == 0, first, odd)
    vec = q3[QUARTER - 40 : QUARTER]

    act, w2, qx, k, v, out, nq, iq, nk, ik = pl.pallas_call(
        qkv_attend_kernel,
        out_shape=(
            shape(2 * rows, D), shape(D, 3 * D), shape(H, rows, 128),
            shape(3, 2 * rows, 128), shape(3, 2 * rows, 128), shape(3, rows, 128, dtype=F32),
            shape(rows, D, dtype=F32), shape(rows, D, dtype=F32),
            shape(2 * rows, D, dtype=F32), shape(2 * rows, D, dtype=F32),
        ),
        scratch_shapes=[vmem(ROW_OUT, 128, dtype=F32), vmem(3, rows, 128)],
        name="qkv_attend",
    )(xo, xt, q0[:ROW_OUT], vec)
    cot = across(cotangent)
    y, gmid, gattn, da, dv = pl.pallas_call(
        mlp_kernel,
        out_shape=(
            shape(rows, D), shape(rows, D, dtype=F32), shape(rows, D),
            shape(PAD_A, 128), shape(24, 128, dtype=F32),
        ),
        scratch_shapes=[
            vmem(ROWS_A + 40, 128, dtype=F32), vmem(D, D), vmem(D, FF), vmem(FF, D), vmem(rows, D),
            vmem(rows, D, dtype=F32), vmem(rows, D, dtype=F32), vmem(rows, D, dtype=F32),
            vmem(rows, D, dtype=F32), vmem(1, FF, dtype=F32),
        ],
        name="mlp",
    )(xo, out, cot, q0, q1, q2, q3)
    db, go, gt = pl.pallas_call(
        attend_back_kernel,
        out_shape=(shape(PAD_B, 128), shape(rows, D, dtype=F32), shape(rows, D)),
        scratch_shapes=[
            vmem(ROW_OUT, 128, dtype=F32), vmem(3, rows, 128), vmem(3, rows, 128, dtype=F32),
            vmem(3, 2 * rows, 128, dtype=F32), vmem(3, 2 * rows, 128), vmem(2 * rows, 3 * D),
            vmem(128, 128, dtype=F32),
        ],
        name="attend_back",
    )(xo, xt, act, w2, qx, k, v, out, nq, iq, nk, ik, vec, gattn, gmid, dv)

    def give_back(mine):
        kept, sent = mine[:own_len], mine[own_len:]
        got = swap(sent, 2)
        return jnp.where(x == 0, jnp.stack([kept, got]), jnp.stack([got, kept]))

    out_tokens = give_back(y)
    grad_tokens = give_back((go + swap(gt, 1).astype(F32)).astype(BF16))

    bits = []
    b = 1
    while b < replicas:
        bits.append(b)
        b *= 2
    moves = [(swap, 1, c), (swap, 2, x)] + [(swap_rep, b, (rep // b) % 2) for b in bits]

    def reduce_all(part):
        for move, bit, side in moves[:-1]:
            n = part.shape[0] // 2
            sent = lax.dynamic_slice_in_dim(part, (1 - side) * n, n, 0)
            kept = lax.dynamic_slice_in_dim(part, side * n, n, 0)
            part = (kept.astype(F32) + move(sent, bit).astype(F32)).astype(BF16)
        move, bit, side = moves[-1]
        part = (part.astype(F32) + move(part, bit).astype(F32)).astype(BF16)
        for move, bit, side in moves[:-1][::-1]:
            got = move(part, bit)
            part = jnp.where(side == 0, jnp.concatenate([part, got]), jnp.concatenate([got, part]))
        return part

    sum_a = reduce_all(da)
    sum_b = reduce_all(db)
    full = jnp.concatenate([sum_b[:ROW_OUT], sum_a[:ROWS_A], sum_b[ROW_OUT : ROW_OUT + 40]]).astype(F32)
    grad = lax.dynamic_slice_in_dim(full, place * QUARTER, QUARTER, 0).reshape(-1)
    momentum_new = MOMENT * momentum + grad
    weight_new = weight - rate[0] * (grad + MOMENT * momentum_new)
    step_value = step[0].astype(F32)
    decay = jnp.minimum(DECAY_MAX, (1.0 + step_value) / (10.0 + step_value))
    average_new = decay * average + (1.0 - decay) * weight_new
    return (
        out_tokens, grad_tokens, grad, momentum_new, average_new, weight_new, weight_new.astype(BF16),
    )


def solution(mesh):
    tok, flat = P("replica", "group", None), P("group")

    def body(*args):
        return per_device(*args, replicas=mesh.shape["replica"])

    return jax.shard_map(
        body,
        mesh=mesh,
        in_specs=(tok, tok, flat, flat, flat, P(), P()),
        out_specs=(tok, tok, flat, flat, flat, flat, flat),
        check_vma=False,
    )
```

```python
import jax
import jax.numpy as jnp
from jax import lax
from jax.experimental import pallas as pl
from jax.experimental.pallas import tpu as pltpu
from jax.sharding import PartitionSpec as P


D = 384
DH = 64
FF = 1536
EPSILON = 1e-06
MOMENT = 0.9
DECAY_MAX = 0.999
INV_ROOT_TWO = 0.7071067811865476
INV_ROOT_TAU = 0.3989422804014327
SCALE = DH ** (-0.5)

ROW_OUT = 3456
ROW_FC1 = 4608
ROW_FC2 = 9216
ROW_VEC = 13824
QUARTER = 3466
PAD_Q = 3488
VEC_AT = ROW_VEC - 3 * QUARTER
SLOT = 3584
HALF = SLOT // 2
BLOCK = SLOT // 4
PAIR = 3 * D
LATE = 2 * PAIR + 64
EARLY_HALF = PAIR // 2
LATE_HALF = LATE // 2
VEC_IN_LATE = VEC_AT - (SLOT - LATE_HALF)

F32 = jnp.float32
BF16 = jnp.bfloat16


def dot_nn(a, b):
    return lax.dot_general(a, b, (((1,), (0,)), ((), ())), preferred_element_type=F32)


def dot_nt(a, b):
    return lax.dot_general(a, b, (((1,), (1,)), ((), ())), preferred_element_type=F32)


def dot_tn(a, b):
    return lax.dot_general(a, b, (((0,), (0,)), ((), ())), preferred_element_type=F32)


def row_of(vec, start, count):
    return jnp.concatenate([vec[start + i : start + i + 1] for i in range(count)], axis=1)


def norm(values):
    center = values - jnp.mean(values, -1, keepdims=True)
    inv = lax.rsqrt(jnp.mean(center * center, -1, keepdims=True) + EPSILON)
    return center * inv, inv


def norm_back(grad_norm, normed, inv):
    inner = jnp.mean(grad_norm * normed, -1, keepdims=True)
    return inv * (grad_norm - jnp.mean(grad_norm, -1, keepdims=True) - normed * inner)


def head_mean_matrix():
    r = lax.broadcasted_iota(jnp.int32, (256, 128), 0)
    c = lax.broadcasted_iota(jnp.int32, (256, 128), 1)
    return jnp.where((r % 128) // DH == c // DH, 1.0 / DH, 0.0).astype(BF16)


def head_mean(x, matrix):
    hi = x.astype(BF16)
    lo = (x - hi.astype(F32)).astype(BF16)
    return dot_nn(jnp.concatenate([hi, lo], axis=1), matrix)


def lane_head(rows, h):
    lane = lax.broadcasted_iota(jnp.int32, (rows, 128), 1)
    return (lane // DH) == h, lane - DH * (1 - h)


def spread(hi_of):
    hi = hi_of.astype(BF16)
    rest = hi_of - hi.astype(F32)
    mid = rest.astype(BF16)
    return hi, mid, (rest - mid.astype(F32)).astype(BF16)


def in_lanes(other, terms):
    out = jnp.where(other == 2, terms[2], BF16(0.0))
    return jnp.where(other == 0, terms[0], jnp.where(other == 1, terms[1], out))


def fetch(place, sources, window, dst, sem):
    for i, src in enumerate(sources):
        @pl.when(place == i)
        def _(src=src):
            pltpu.make_async_copy(src.at[window], dst, sem).start()


def arrive(src, window, dst, sem):
    pltpu.make_async_copy(src.at[window], dst, sem).wait()


def pair_gains(vec):
    gains = vec[15:16]
    return (
        jnp.concatenate([gains[:, :DH], gains[:, :DH]], axis=1),
        jnp.concatenate([gains[:, DH:], gains[:, DH:]], axis=1),
    )


def qkv_attend_kernel(
    t0, t1, t2, t3, vec_in, own, beside, w1_in, c1_in,
    act_ref, w2_ref, qx_ref, k_ref, v_ref, out_ref, nq_ref, iq_ref, nk_ref, ik_ref, vec_ref,
    raw, flat, q_s, sem,
):
    own_len = t0.shape[0]
    rows = 2 * own_len
    step = own_len
    place = lax.axis_index("group")
    q0_rows = pl.ds(0, ROW_OUT)
    fetch(place, (own, beside, w1_in, c1_in), q0_rows, raw, sem)
    vec = vec_in[...].astype(F32)[2:42]
    vec_ref[...] = vec
    gain_one, bias_one, bias_qkv = row_of(vec, 0, 3), row_of(vec, 3, 3), row_of(vec, 6, 9)
    gain_q, gain_k = pair_gains(vec)

    for i, ref in enumerate((t0, t1, t2, t3)):
        n, _ = norm(ref[...].astype(F32))
        act_ref[step * i : step * i + step, :] = (n * gain_one + bias_one).astype(BF16)

    arrive(own, q0_rows, raw, sem)
    flat[...] = raw[...].astype(F32)
    for j in range(9):
        p, t = j % 3, j // 3
        w2_ref[p, :, 128 * t : 128 * t + 128] = flat[pl.ds(j, D, stride=9), :].astype(BF16)
    matrix = head_mean_matrix()

    def heads(x, gain, n_ref, i_ref, p):
        c = x - head_mean(x, matrix)
        inv = lax.rsqrt(head_mean(c * c, matrix) + EPSILON)
        n = c * inv
        n_ref[p] = n
        i_ref[p] = inv
        return n * gain

    def bias(p, t):
        return bias_qkv[:, D * t + 128 * p : D * t + 128 * p + 128]

    for p in range(3):
        x = dot_nn(act_ref[...], w2_ref[p, :, 128:])
        y = heads(x[:, :128] + bias(p, 1), gain_k, nk_ref, ik_ref, p)
        k_ref[p] = y.astype(BF16)
        v_ref[p] = (x[:, 128:] + bias(p, 2)).astype(BF16)
        x = dot_nn(act_ref[0:rows, :], w2_ref[p, :, :128]) + bias(p, 0)
        q_s[p] = heads(x, gain_q, nq_ref, iq_ref, p).astype(BF16) * BF16(SCALE)

    def attend(p, c):
        q, k, v = q_s[p], k_ref[p], v_ref[p]
        parts = []
        for h in range(2):
            mine, _ = lane_head(2 * rows, h)
            own_l, other = lane_head(rows, h)
            qm = jnp.where(own_l, q, BF16(0.0))
            e = jnp.exp(dot_nt(qm, k)).astype(BF16)
            o = dot_nn(e, jnp.where(mine, v, BF16(1.0)))
            parts.append(o / pltpu.roll(o, DH, 1))
            qx_ref[p, h] = jnp.where(own_l, qm, in_lanes(other, spread(-jnp.log(o))))
        own_l, _ = lane_head(rows, 0)
        out_ref[p] = jnp.where(own_l, parts[0], parts[1])
        return c

    lax.fori_loop(0, 3, attend, 0)


OUT_HEAD = (4, 3, 3)
FC1_HEAD = tuple((2 * QUARTER - ROW_FC1 - j + 11) // 12 for j in range(12))
FC2_HEAD = (3 * QUARTER - ROW_FC2) // 3


def mlp_kernel(
    t0, t1, o_ref, cot0, cot1, own, beside, w1_in, c1_in, w2_in, c2_in,
    yk_ref, ys_ref, gmid_ref, gattn_ref, keep_ref, send_ref, wout_ref,
    raw, raw0, quarters, slots, wo_s, w1_s, w2_s, x_s, act_s, n_s, gn_s, y_s, db1_s, cot_s, sems,
):
    own_len = t0.shape[0]
    place = lax.axis_index("group")
    core = place % 2
    all_rows, tail = pl.ds(0, PAD_Q), pl.ds(ROW_OUT, 16)
    fetch(place, (own, beside, w1_in, c1_in), tail, raw0, sems.at[0])
    fetch(place, (beside, own, c2_in, w2_in), all_rows, raw.at[0], sems.at[1])
    fetch(place, (w1_in, c1_in, own, beside), all_rows, raw.at[1], sems.at[2])
    fetch(place, (c2_in, w2_in, beside, own), all_rows, raw.at[2], sems.at[3])
    x_s[0:own_len, :] = t0[...].astype(F32)
    x_s[own_len:, :] = t1[...].astype(F32)
    cot_s[0:own_len, :] = cot0[...]
    cot_s[own_len:, :] = cot1[...]
    attn = jnp.concatenate([o_ref[p].astype(BF16) for p in range(3)], axis=1)
    arrive(own, tail, raw0, sems.at[0])
    for i in range(3):
        arrive(own, all_rows, raw.at[i], sems.at[1 + i])
        quarters[i] = raw[i].astype(F32)
    first = raw0[...].astype(F32)
    vec = quarters[2, VEC_AT : VEC_AT + 40, :]
    bias_out, gain_two, bias_two = row_of(vec, 16, 3), row_of(vec, 19, 3), row_of(vec, 22, 3)
    bias_fc1, bias_fc2 = row_of(vec, 25, 12), row_of(vec, 37, 3)
    q1, q2, q3 = quarters.at[0], quarters.at[1], quarters.at[2]
    for j in range(3):
        n = OUT_HEAD[j]
        top = jnp.concatenate([first[3 * i + j : 3 * i + j + 1] for i in range(n)], axis=0)
        rest = q1[pl.ds(3 * n + j - 10, D - n, stride=3), :]
        wo_s[:, 128 * j : 128 * j + 128] = jnp.concatenate([top, rest], axis=0).astype(BF16)
        top = q2[pl.ds(ROW_FC2 - 2 * QUARTER + j, FC2_HEAD, stride=3), :]
        rest = q3[pl.ds(j, FF - FC2_HEAD, stride=3), :]
        w2_s[:, 128 * j : 128 * j + 128] = jnp.concatenate([top, rest], axis=0).astype(BF16)
    for j in range(12):
        n = FC1_HEAD[j]
        top = q1[pl.ds(ROW_FC1 - QUARTER + j, n, stride=12), :]
        rest = q2[pl.ds(ROW_FC1 - 2 * QUARTER + 12 * n + j, D - n, stride=12), :]
        w1_s[:, 128 * j : 128 * j + 128] = jnp.concatenate([top, rest], axis=0).astype(BF16)

    mid = x_s[...] + dot_nn(attn, wo_s[...]) + bias_out
    n, inv = norm(mid)
    n_s[...] = n
    act_s[...] = (n * gain_two + bias_two).astype(BF16)
    y_s[...] = mid + bias_fc2
    gn_s[...] = jnp.zeros_like(gn_s)
    width = 256
    for f in range(FF // width):
        at = f * width
        w1 = w1_s[:, at : at + width]
        w2 = w2_s[at : at + width, :]
        x = dot_nn(act_s[...], w1) + bias_fc1[:, at : at + width]
        phi = 0.5 * (1.0 + lax.erf(x * INV_ROOT_TWO))
        hid = (x * phi).astype(BF16)
        slope = phi + x * jnp.exp(-0.5 * x * x) * INV_ROOT_TAU
        gb = (dot_nt(cot_s[...], w2) * slope).astype(BF16)
        y_s[...] += dot_nn(hid, w2)
        gn_s[...] += dot_nt(gb, w1)
        dw2 = dot_tn(hid, cot_s[...])
        cut = min(max(FC2_HEAD - at, 0), width)
        for j in range(3):
            piece = dw2[:, 128 * j : 128 * j + 128]
            if cut > 0:
                slots[pl.ds(SLOT + ROW_FC2 - 2 * QUARTER + 3 * at + j, cut, stride=3), :] = piece[:cut]
            if cut < width:
                base = 2 * SLOT + 3 * (at + cut - FC2_HEAD) + j
                slots[pl.ds(base, width - cut, stride=3), :] = piece[cut:]
        dw1 = dot_tn(act_s[...], gb)
        for i in range(width // 128):
            j = at // 128 + i
            n1 = FC1_HEAD[j]
            piece = dw1[:, 128 * i : 128 * i + 128]
            slots[pl.ds(ROW_FC1 - QUARTER + j, n1, stride=12), :] = piece[:n1]
            base = SLOT + ROW_FC1 - 2 * QUARTER + 12 * n1 + j
            slots[pl.ds(base, D - n1, stride=12), :] = piece[n1:]
        db1_s[:, at : at + width] = jnp.sum(gb.astype(F32), 0, keepdims=True)
    yk_ref[...] = y_s[0:own_len, :].astype(BF16)
    ys_ref[...] = y_s[own_len:, :].astype(BF16)
    gn = gn_s[...]
    cot = cot_s[...].astype(F32)
    gmid = cot + norm_back(gn * gain_two, n_s[...], inv)
    gmid_ref[...] = gmid
    gproj = gmid.astype(BF16)
    gattn = dot_nt(gproj, wo_s[...]).astype(BF16)
    for p in range(3):
        gattn_ref[p] = gattn[:, 128 * p : 128 * p + 128]
    dwo = dot_tn(attn, gproj)
    for j in range(3):
        n0 = OUT_HEAD[j]
        piece = dwo[:, 128 * j : 128 * j + 128]
        slots[pl.ds(QUARTER + j, n0, stride=3), :] = piece[:n0]
        slots[pl.ds(3 * n0 + j - 10, D - n0, stride=3), :] = piece[n0:]
    slots[QUARTER + 10 : SLOT, :] = jnp.zeros((SLOT - QUARTER - 10, 128), F32)
    slots[SLOT + QUARTER : 2 * SLOT, :] = jnp.zeros((SLOT - QUARTER, 128), F32)
    slots[2 * SLOT + VEC_AT : 3 * SLOT, :] = jnp.zeros((SLOT - VEC_AT, 128), F32)

    def put(at, row):
        for i in range(row.shape[1] // 128):
            slots[2 * SLOT + VEC_AT + at + i : 2 * SLOT + VEC_AT + at + i + 1, :] = row[:, 128 * i : 128 * i + 128]

    put(16, jnp.sum(gproj.astype(F32), 0, keepdims=True))
    put(19, jnp.sum(gn * n_s[...], 0, keepdims=True))
    put(22, jnp.sum(gn, 0, keepdims=True))
    put(25, db1_s[...])
    put(37, jnp.sum(cot, 0, keepdims=True))
    wout_ref[0:10, :] = slots[QUARTER : QUARTER + 10, :].astype(BF16)
    wout_ref[10:, :] = jnp.zeros((54, 128), BF16)

    def deal(odd, even):
        for i in range(2):
            odd[i * SLOT : i * SLOT + SLOT, :] = slots[2 * i * SLOT : 2 * i * SLOT + SLOT, :].astype(BF16)
            at = SLOT + i * HALF
            even[i * SLOT : i * SLOT + HALF, :] = slots[at : at + HALF, :].astype(BF16)
            even[i * SLOT + HALF : i * SLOT + SLOT, :] = jnp.zeros((HALF, 128), BF16)

    @pl.when(core == 0)
    def _():
        deal(send_ref, keep_ref)

    @pl.when(core != 0)
    def _():
        deal(keep_ref, send_ref)


def pairs_back_kernel(
    act_ref, qx_ref, k_ref, v_ref, out_ref, nq_ref, iq_ref, nk_ref, ik_ref, vec_ref, ga_ref, *refs, pair,
):
    if pair == 0:
        _, _, g_ref, sums_ref, keep_any, send_any, part, sems = refs
    elif pair == 1:
        g_ref, sums_ref, part = refs
    else:
        (t0, t1, t2, t3, w2_ref, gmid_ref, wout_ref, g0_ref, g1_ref, sums0, sums1, part1_ref,
         g_ref, sums_ref, go_ref, gt_ref, keep_ref, send_ref, part, vrow) = refs
    core = lax.axis_index("group") % 2
    rows = ga_ref.shape[0]
    gain_q, gain_k = pair_gains(vec_ref[...])
    matrix = head_mean_matrix()
    k, v, ga = k_ref[...], v_ref[...], ga_ref[...]
    inner = -float(DH) * head_mean(ga.astype(F32) * out_ref[...], matrix)
    terms = spread(pltpu.roll(inner, DH, 1))
    gq_t = jnp.zeros((128, rows), F32)
    gk = jnp.zeros((2 * rows, 128), F32)
    gv = jnp.zeros((2 * rows, 128), F32)
    for h in range(2):
        mine, other_all = lane_head(2 * rows, h)
        own, other = lane_head(rows, h)
        ones = jnp.where((other_all >= 0) & (other_all <= 2), 1.0, 0.0).astype(BF16)
        qx = qx_ref[h]
        gax = jnp.where(own, ga, in_lanes(other, terms))
        prob = jnp.exp(dot_nt(jnp.where(mine, k, ones), qx))
        gprob = dot_nt(jnp.where(mine, v, ones), gax)
        gs = (prob * gprob).astype(BF16)
        gv = gv + dot_nn(prob.astype(BF16), jnp.where(own, ga, BF16(0.0)))
        gk = gk + dot_nn(gs, jnp.where(own, qx, BF16(0.0)))
        gq_t = gq_t + dot_tn(jnp.where(mine, k, BF16(0.0)), gs)
    gq = (gq_t.T * SCALE).astype(BF16).astype(F32)
    gk = gk.astype(BF16).astype(F32)

    def head_back(u, n, inv, gain):
        dn = u * gain
        return (inv * (dn - head_mean(dn, matrix) - n * head_mean(dn * n, matrix))).astype(BF16)

    def total(a):
        return jnp.sum(a, 0, keepdims=True)

    gq_b = head_back(gq, nq_ref[...], iq_ref[...], gain_q)
    gk_b = head_back(gk, nk_ref[...], ik_ref[...], gain_k)
    gv_b = gv.astype(BF16)
    g_ref[0:rows, 0:128] = gq_b
    g_ref[rows:, 0:128] = jnp.zeros((rows, 128), BF16)
    g_ref[:, 128:256] = gk_b
    g_ref[:, 256:384] = gv_b
    sums_ref[0:1, :] = total(gq_b.astype(F32))
    sums_ref[1:2, :] = total(gk_b.astype(F32))
    sums_ref[2:3, :] = total(gv_b.astype(F32))
    sums_ref[3:4, :] = total(gq * nq_ref[...])
    sums_ref[4:5, :] = total(gk * nk_ref[...])
    sums_ref[5:8, :] = jnp.zeros((3, 128), F32)
    dwq = dot_tn(act_ref[0:rows, :], gq_b).astype(BF16)
    dwkv = dot_tn(act_ref[...], g_ref[:, 128:384]).astype(BF16)
    part[0:D, :] = dwq
    part[D : 2 * D, :] = dwkv[:, :128]
    part[2 * D : PAIR, :] = dwkv[:, 128:]
    if pair == 0:
        def move(into):
            copies = [
                pltpu.make_async_copy(
                    part.at[pl.ds(h * EARLY_HALF, EARLY_HALF)],
                    into.at[pl.ds(h * SLOT + HALF, EARLY_HALF)], sems.at[h],
                )
                for h in range(2)
            ]
            for copy in copies:
                copy.start()
            for copy in copies:
                copy.wait()

        @pl.when(core == 0)
        def _():
            move(keep_any)

        @pl.when(core != 0)
        def _():
            move(send_any)
    if pair < 2:
        return
    own_len = t0.shape[0]
    gain_one = row_of(vec_ref[...], 0, 3)
    d_gain = jnp.zeros((1, D), F32)
    d_bias = jnp.zeros((1, D), F32)
    for i, ref in enumerate((t0, t1, t2, t3)):
        at = own_len * i
        cols = slice(0, D) if i < 2 else slice(128, D)
        u = sum(
            dot_nt(g[at : at + own_len, cols], w2_ref[p, :, cols])
            for p, g in enumerate((g0_ref, g1_ref, g_ref))
        )
        n, inv = norm(ref[...].astype(F32))
        d_gain = d_gain + total(u * n)
        d_bias = d_bias + total(u)
        back = norm_back(u * gain_one, n, inv)
        if i < 2:
            go_ref[at : at + own_len, :] = gmid_ref[at : at + own_len, :] + back
        else:
            gt_ref[at - rows : at - rows + own_len, :] = back.astype(BF16)
    for i in range(3):
        vrow[i : i + 1, :] = d_gain[:, 128 * i : 128 * i + 128]
        vrow[3 + i : 4 + i, :] = d_bias[:, 128 * i : 128 * i + 128]
    sums = (sums0[...], sums1[...], sums_ref[...])
    for p, s in enumerate(sums):
        for t in range(3):
            vrow[6 + 3 * t + p : 7 + 3 * t + p, :] = s[t : t + 1, :]
    dgq = sums[0][3:4, :] + sums[1][3:4, :] + sums[2][3:4, :]
    dgk = sums[0][4:5, :] + sums[1][4:5, :] + sums[2][4:5, :]
    low, _ = lane_head(1, 0)
    vrow[15:16, :] = jnp.where(low, dgq + pltpu.roll(dgq, DH, 1), dgk + pltpu.roll(dgk, DH, 1))

    def deal(matrix_to, vector_to):
        matrix_to[0:PAIR, :] = part1_ref[...]
        matrix_to[PAIR : 2 * PAIR, :] = part[...]
        matrix_to[2 * PAIR :, :] = wout_ref[...]
        vector_to[...] = jnp.zeros((LATE, 128), BF16)
        vector_to[VEC_IN_LATE - 2 : VEC_IN_LATE + 30, :] = jnp.concatenate(
            [jnp.zeros((2, 128), F32), vrow[...], jnp.zeros((14, 128), F32)], axis=0
        ).astype(BF16)

    @pl.when(core == 0)
    def _():
        deal(keep_ref, send_ref)

    @pl.when(core != 0)
    def _():
        deal(send_ref, keep_ref)


def finish_kernel(cat, got, out, slot, *, bits):
    place, rep = lax.axis_index("group"), lax.axis_index("replica")
    y = jnp.minimum(rep & bits[0], 1)
    t0, t1 = jnp.minimum(rep & bits[1], 1), jnp.minimum(rep & bits[-1], 1)
    t = jnp.where(place % 2 == 0, t0, t1)
    one, two = jnp.where(place % 2 == 0, 2, 1), jnp.where(place % 2 == 0, 1, 2)
    mine = 2 * y + t
    spots = (mine, mine ^ one, mine ^ two, 3 - mine)

    def blocks(into):
        for i in range(4):
            src = (cat, got)[i // 2]
            off = pl.multiple_of(spots[i] * BLOCK, 16)
            into[pl.ds(off, BLOCK), :] = src[(i % 2) * BLOCK : (i % 2) * BLOCK + BLOCK, :].astype(F32)

    @pl.when(place != 0)
    def _():
        blocks(out)

    @pl.when(place == 0)
    def _():
        blocks(slot)

        def rows(start, stop):
            late = start >= PAIR
            half, skip, base = (LATE_HALF, EARLY_HALF, PAIR) if late else (EARLY_HALF, 0, 0)
            pieces = []
            while start < stop:
                h = (start - base) // half
                end = min(stop, base + (h + 1) * half)
                row = h * HALF + skip + start - base - h * half
                pieces.append(slot[row : row + end - start, :])
                start = end
            return pieces[0] if len(pieces) == 1 else jnp.concatenate(pieces, axis=0)

        for p in range(3):
            for t in range(3):
                out[pl.ds(3 * t + p, D, stride=9), :] = rows(PAIR * p + D * t, PAIR * p + D * t + D)
        out[ROW_OUT : ROW_OUT + 10, :] = rows(3 * PAIR, 3 * PAIR + 10)


def shape(*dims, dtype=BF16):
    return jax.ShapeDtypeStruct(dims, dtype)


def vmem(*dims, dtype=BF16):
    return pltpu.VMEM(dims, dtype)


class Plan:
    def __init__(self, replicas):
        self.replicas = replicas
        self.bits = []
        while 2 ** len(self.bits) < replicas:
            self.bits.append(2 ** len(self.bits))
        self.thirds = (self.bits[1], self.bits[-1])
        self.rest = list(zip(self.bits[2:], self.bits[-2:0:-1]))

    def swap(self, a, dims, places=(0, 1, 2, 3)):
        pairs = []
        for rep in range(self.replicas):
            for place in places:
                dim = dims[place % 2]
                if dim is not None:
                    to = (rep, place ^ 2) if dim == "x" else (rep ^ dim, place)
                    pairs.append((place * self.replicas + rep, to[1] * self.replicas + to[0]))
        return lax.ppermute(a, ("group", "replica"), pairs)


def whole(a):
    return pl.BlockSpec(a.shape, lambda i, n=len(a.shape): (0,) * n)


ANY = pl.BlockSpec(memory_space=pl.ANY)


def call(kernel, args, outs, scratch=(), specs=None, out_specs=None, flops=0, aliases={}):
    specs = specs or [None] * len(args)
    out_specs = out_specs or [None] * len(outs)
    return pl.pallas_call(
        kernel,
        out_shape=outs,
        grid=(1,),
        in_specs=[s or whole(a) for s, a in zip(specs, args)],
        out_specs=tuple(s or whole(o) for s, o in zip(out_specs, outs)),
        scratch_shapes=list(scratch),
        cost_estimate=pl.CostEstimate(flops=flops, transcendentals=0, bytes_accessed=0) if flops else None,
        input_output_aliases=aliases,
    )(*args)


def per_device(tokens, cotangent, weight, momentum, average, rate, step, replicas):
    _, own_len, _ = tokens.shape
    rows = 2 * own_len
    x, c = lax.axis_index("group") // 2, lax.axis_index("group") % 2
    plan = Plan(replicas)

    place, rep = lax.axis_index("group"), lax.axis_index("replica")
    y = jnp.minimum(rep & plan.bits[0], 1)
    t = jnp.minimum(rep & jnp.where(c == 0, plan.thirds[0], plan.thirds[1]), 1)
    at_1 = [b * SLOT for b in (jnp.where(c == 0, y, x), jnp.where(c == 0, 1 - y, 1 - x))]
    at_3 = [jnp.where(c == 0, b * LATE_HALF, 0) for b in (y, 1 - y)]
    at_4 = [b * HALF for b in (jnp.where(c == 0, 1 - x, y), jnp.where(c == 0, x, 1 - y))]
    at_5 = [b * BLOCK for b in (t, 1 - t)]

    def move(a, pairs):
        return lax.ppermute(a, "group", pairs)

    def beside_of(a):
        return move(a, [(0, 1), (1, 0), (2, 3), (3, 2)])

    def over_x(a):
        return move(a, [(0, 2), (1, 3), (2, 0), (3, 1)])

    def pick(a, i):
        return lax.dynamic_index_in_dim(a, i, 0, keepdims=False)

    t1 = over_x(pick(tokens, 1 - x))
    t0 = pick(tokens, x)
    own = jnp.pad(weight.reshape(QUARTER, 128).astype(BF16), ((0, PAD_Q - QUARTER), (0, 0)))
    tail = own[VEC_AT - 2 : VEC_AT + 46]
    vec_x = move(tail, [(1, 3), (3, 1)])
    w1 = move(own, [(0, 2), (2, 0)])
    beside = beside_of(own)
    w2 = move(own, [(1, 3), (3, 1)])
    cot1 = over_x(pick(cotangent, 1 - x))
    cot0 = pick(cotangent, x)
    vec_b = jnp.where(place == 1, vec_x, tail)
    vec_b = jnp.where(c == 1, vec_b, beside_of(vec_b))
    t2, t3 = beside_of(t0), beside_of(t1)
    c1 = beside_of(w1)
    c2 = beside_of(w2)

    tok = [None] * 4
    act, w_cols, qx, k, v, out, nq, iq, nk, ik, vec = call(
        qkv_attend_kernel, (t0, t1, t2, t3, vec_b, own, beside, w1, c1),
        (
            shape(2 * rows, D), shape(3, D, D), shape(3, 2, rows, 128),
            shape(3, 2 * rows, 128), shape(3, 2 * rows, 128), shape(3, rows, 128, dtype=F32),
            shape(3, rows, 128, dtype=F32), shape(3, rows, 128, dtype=F32),
            shape(3, 2 * rows, 128, dtype=F32), shape(3, 2 * rows, 128, dtype=F32),
            shape(40, 128, dtype=F32),
        ),
        [
            vmem(ROW_OUT, 128), vmem(ROW_OUT, 128, dtype=F32), vmem(3, rows, 128),
            pltpu.SemaphoreType.DMA,
        ],
        specs=tok + [None] + [ANY] * 4, flops=10 ** 10,
    )
    yk, ys, gmid, gattn, keep, send, wout = call(
        mlp_kernel, (t0, t1, out, cot0, cot1, own, beside, w1, c1, w2, c2),
        (
            shape(own_len, D), shape(own_len, D), shape(rows, D, dtype=F32), shape(3, rows, 128),
            shape(2 * SLOT, 128), shape(2 * SLOT, 128), shape(64, 128),
        ),
        [
            vmem(3, PAD_Q, 128), vmem(16, 128), vmem(3, PAD_Q, 128, dtype=F32),
            vmem(3 * SLOT, 128, dtype=F32), vmem(D, D), vmem(D, FF), vmem(FF, D),
            vmem(rows, D, dtype=F32), vmem(rows, D), vmem(rows, D, dtype=F32),
            vmem(rows, D, dtype=F32), vmem(rows, D, dtype=F32), vmem(1, FF, dtype=F32), vmem(rows, D),
            pltpu.SemaphoreType.DMA((4,)),
        ],
        specs=[None] * 5 + [ANY] * 6, flops=10 ** 10,
    )

    def add(a, b):
        return (a.astype(F32) + b.astype(F32)).astype(BF16)

    def split(at, rows, total):
        return tuple(total(lambda a: lax.dynamic_slice_in_dim(a, at[i], rows, 0)) for i in range(2))

    def tie(a, b):
        return lax.optimization_barrier((a, b))

    def back(pair, first, extra=(), specs=(), outs=(), out_specs=(), scratch=(), aliases={}):
        def one(a):
            dims = tuple(a.shape[1:])
            return pl.BlockSpec((None,) + dims, lambda i, n=len(dims): (pair,) + (0,) * n)

        args = (act, qx, first, v, out, nq, iq, nk, ik, vec, gattn)
        in_specs = [None] + [one(a) for a in args[1:9]] + [None, one(gattn)] + list(specs)
        return call(
            lambda *refs: pairs_back_kernel(*refs, pair=pair), args + tuple(extra),
            (shape(2 * rows, D), shape(8, 128, dtype=F32)) + tuple(outs), scratch,
            specs=in_specs, out_specs=(None, None) + tuple(out_specs), flops=5 * 10 ** 9,
            aliases=aliases,
        )

    got_y = over_x(ys)
    g0, s0, keep, send = back(
        0, k, (keep, send), [ANY] * 2, (shape(2 * SLOT, 128), shape(2 * SLOT, 128)), [ANY] * 2,
        [vmem(PAIR, 128), pltpu.SemaphoreType.DMA((2,))], aliases={11: 2, 12: 3},
    )
    k1, send = tie(k, send)
    arrived = beside_of(send)
    g1, s1, part1 = back(1, k1, outs=(shape(PAIR, 128),), out_specs=(None,))
    kept, sent = split(at_1, SLOT, lambda cut: add(cut(keep), cut(arrived)))
    part1, sent = tie(part1, sent)
    got = plan.swap(sent, (plan.bits[0], "x"))
    extra = (t0, t1, t2, t3, w_cols, gmid, wout, g0, g1, s0, s1, part1)
    _, _, go, gt, keep_l, send_l = back(
        2, k, extra, [None] * 12,
        (shape(rows, D, dtype=F32), shape(rows, D), shape(LATE, 128), shape(LATE, 128)),
        [None] * 4, [vmem(PAIR, 128), vmem(16, 128, dtype=F32)],
    )
    arrived = beside_of(send_l)
    kept_l, sent = split(at_3, LATE_HALF, lambda cut: add(cut(keep_l), cut(arrived)))
    late = add(kept_l, plan.swap(sent, (plan.bits[0], "x")))
    late = jnp.where((c == 1) & (x == 0), BF16(0.0), late)

    def with_late(cut):
        below = jnp.where(c == 0, HALF + EARLY_HALF, SLOT - LATE_HALF)
        zeros = jnp.zeros((SLOT, 128), BF16)
        return add(add(cut(kept), cut(got)), cut(lax.dynamic_update_slice_in_dim(zeros, late, below, 0)))

    kept, sent = split(at_4, HALF, with_late)
    got = plan.swap(sent, ("x", plan.bits[0]))
    kept, sent = split(at_5, BLOCK, lambda cut: add(cut(kept), cut(got)))
    part = add(kept, plan.swap(sent, plan.thirds))
    for dims in plan.rest:
        part = add(part, plan.swap(part, dims))
    cat = jnp.concatenate([part, plan.swap(part, (plan.bits[0], plan.thirds[1]))])
    got = plan.swap(cat, (plan.thirds[0], plan.bits[0]))

    both = (go + beside_of(gt).astype(F32)).astype(BF16)
    got_g = over_x(both[own_len:])

    def given(kept, got):
        first = lax.broadcasted_iota(jnp.int32, tokens.shape, 0) == x
        return jnp.where(first, kept[None], got[None])

    out_tokens = given(yk, got_y)
    grad_tokens = given(both[:own_len], got_g)
    grad = call(
        lambda *refs: finish_kernel(*refs, bits=plan.bits), (cat, got),
        (shape(SLOT, 128, dtype=F32),), [vmem(SLOT, 128, dtype=F32)],
    )[0]
    grad = grad[:QUARTER].reshape(-1)
    momentum_new = MOMENT * momentum + grad
    weight_new = weight - rate[0] * (grad + MOMENT * momentum_new)
    step_value = step[0].astype(F32)
    decay = jnp.minimum(DECAY_MAX, (1.0 + step_value) / (10.0 + step_value))
    average_new = decay * average + (1.0 - decay) * weight_new
    return (
        out_tokens, grad_tokens, grad, momentum_new, average_new, weight_new, weight_new.astype(BF16),
    )


def solution(mesh):
    tok, flat = P("replica", "group", None), P("group")

    def body(*args):
        return per_device(*args, replicas=mesh.shape["replica"])

    return jax.shard_map(
        body,
        mesh=mesh,
        in_specs=(tok, tok, flat, flat, flat, P(), P()),
        out_specs=(tok, tok, flat, flat, flat, flat, flat),
        check_vma=False,
    )
```

```python
import jax
import jax.numpy as jnp
from jax import lax
from jax.experimental import pallas as pl
from jax.experimental.pallas import tpu as pltpu
from jax.sharding import PartitionSpec as P


D = 384
DH = 64
FF = 1536
EPSILON = 1e-06
MOMENT = 0.9
DECAY_MAX = 0.999
INV_ROOT_TWO = 0.7071067811865476
INV_ROOT_TAU = 0.3989422804014327
SCALE = DH ** (-0.5)

ROW_OUT = 3456
ROW_FC1 = 4608
ROW_FC2 = 9216
ROW_VEC = 13824
QUARTER = 3466
PAD_Q = 3488
VEC_AT = ROW_VEC - 3 * QUARTER
SLOT = 3584
HALF = SLOT // 2
BLOCK = SLOT // 4
STEP = 512
PAIR = 3 * D
LATE = 2 * PAIR + 64
EARLY_HALF = PAIR // 2
LATE_HALF = LATE // 2
VEC_IN_LATE = VEC_AT - (SLOT - LATE_HALF)

F32 = jnp.float32
BF16 = jnp.bfloat16


def dot_nn(a, b):
    return lax.dot_general(a, b, (((1,), (0,)), ((), ())), preferred_element_type=F32)


def dot_nt(a, b):
    return lax.dot_general(a, b, (((1,), (1,)), ((), ())), preferred_element_type=F32)


def dot_tn(a, b):
    return lax.dot_general(a, b, (((0,), (0,)), ((), ())), preferred_element_type=F32)


def row_of(vec, start, count):
    return jnp.concatenate([vec[start + i : start + i + 1] for i in range(count)], axis=1)


def norm(values):
    center = values - jnp.mean(values, -1, keepdims=True)
    inv = lax.rsqrt(jnp.mean(center * center, -1, keepdims=True) + EPSILON)
    return center * inv, inv


def norm_back(grad_norm, normed, inv):
    inner = jnp.mean(grad_norm * normed, -1, keepdims=True)
    return inv * (grad_norm - jnp.mean(grad_norm, -1, keepdims=True) - normed * inner)


def head_mean_matrix():
    r = lax.broadcasted_iota(jnp.int32, (256, 128), 0)
    c = lax.broadcasted_iota(jnp.int32, (256, 128), 1)
    return jnp.where((r % 128) // DH == c // DH, 1.0 / DH, 0.0).astype(BF16)


def head_mean(x, matrix):
    hi = x.astype(BF16)
    lo = (x - hi.astype(F32)).astype(BF16)
    return dot_nn(jnp.concatenate([hi, lo], axis=1), matrix)


def lane_head(rows, h):
    lane = lax.broadcasted_iota(jnp.int32, (rows, 128), 1)
    return (lane // DH) == h, lane - DH * (1 - h)


def spread(hi_of):
    hi = hi_of.astype(BF16)
    rest = hi_of - hi.astype(F32)
    mid = rest.astype(BF16)
    return hi, mid, (rest - mid.astype(F32)).astype(BF16)


def in_lanes(other, terms):
    out = jnp.where(other == 2, terms[2], BF16(0.0))
    return jnp.where(other == 0, terms[0], jnp.where(other == 1, terms[1], out))


def fetch(place, sources, window, dst, sem):
    for i, src in enumerate(sources):
        @pl.when(place == i)
        def _(src=src):
            pltpu.make_async_copy(src.at[window], dst, sem).start()


def arrive(src, window, dst, sem):
    pltpu.make_async_copy(src.at[window], dst, sem).wait()


def pair_gains(vec):
    gains = vec[15:16]
    return (
        jnp.concatenate([gains[:, :DH], gains[:, :DH]], axis=1),
        jnp.concatenate([gains[:, DH:], gains[:, DH:]], axis=1),
    )


def qkv_attend_kernel(
    t0, t1, t23, vec_in, own, beside, w1_in, c1_in, *refs,
):
    w2_out, attn_ref, t01_out, tok_out, q2_out, q13_out, tail_out = refs[:7]
    per_pair = [refs[7 + 10 * p : 17 + 10 * p] for p in range(3)]
    raw, flat, q_s, act_ref, qx_ref, k_ref, v_ref, out_ref, sem, sems, w2_ref, nq, iq, nk, ik, vec_s = refs[37:]
    own_len = t0.shape[0]
    rows = 2 * own_len
    step = own_len
    t2, t3 = t23.at[pl.ds(0, own_len)], t23.at[pl.ds(own_len, own_len)]
    place = lax.axis_index("group")
    q0_rows, all_rows, tail = pl.ds(0, ROW_OUT), pl.ds(0, PAD_Q), pl.ds(ROW_OUT, 16)
    everything = (own, beside, w1_in, c1_in)
    fetch(place, everything, q0_rows, raw, sem)
    fetch(place, everything, tail, tail_out, sems.at[0])
    fetch(place, (w1_in, c1_in, own, beside), all_rows, q2_out, sems.at[1])
    fetch(place, (beside, own, beside, own), all_rows, q13_out, sems.at[2])
    passed = [
        pltpu.make_async_copy(src, dst, sems.at[3 + i])
        for i, (src, dst) in enumerate((
            (t0, t01_out.at[pl.ds(0, own_len)]), (t1, t01_out.at[pl.ds(own_len, own_len)]),
            (t0, tok_out.at[pl.ds(0, own_len)]), (t1, tok_out.at[pl.ds(own_len, own_len)]),
            (t23, tok_out.at[pl.ds(rows, rows)]),
        ))
    ]
    for copy in passed:
        copy.start()
    vec = vec_in[...].astype(F32)[2:42]
    vec_s[...] = vec

    def leave(i, src, dst):
        copy = pltpu.make_async_copy(src, dst, sems.at[i])
        copy.start()
        passed.append(copy)

    gain_one, bias_one, bias_qkv = row_of(vec, 0, 3), row_of(vec, 3, 3), row_of(vec, 6, 9)
    gain_q, gain_k = pair_gains(vec)

    for i, ref in enumerate((t0, t1, t2, t3)):
        n, _ = norm(ref[...].astype(F32))
        act_ref[step * i : step * i + step, :] = (n * gain_one + bias_one).astype(BF16)

    arrive(own, q0_rows, raw, sem)
    flat[...] = raw[...].astype(F32)
    for j in range(9):
        p, t = j % 3, j // 3
        w2_ref[p, :, 128 * t : 128 * t + 128] = flat[pl.ds(j, D, stride=9), :].astype(BF16)
    matrix = head_mean_matrix()

    def heads(x, gain, n_ref, i_ref):
        c = x - head_mean(x, matrix)
        inv = lax.rsqrt(head_mean(c * c, matrix) + EPSILON)
        n = c * inv
        n_ref[...] = n.astype(BF16)
        i_ref[...] = inv.astype(BF16)
        return n * gain

    def bias(p, t):
        return bias_qkv[:, D * t + 128 * p : D * t + 128 * p + 128]

    for p in range(3):
        x = dot_nn(act_ref[...], w2_ref[p, :, 128:])
        y = heads(x[:, :128] + bias(p, 1), gain_k, nk.at[p], ik.at[p])
        k_ref[p] = y.astype(BF16)
        v_ref[p] = (x[:, 128:] + bias(p, 2)).astype(BF16)
        x = dot_nn(act_ref[0:rows, :], w2_ref[p, :, :128]) + bias(p, 0)
        q_s[p] = heads(x, gain_q, nq.at[p], iq.at[p]).astype(BF16) * BF16(SCALE)
        early = (act_ref if p == 0 else None, None, k_ref.at[p], v_ref.at[p], None, nq.at[p], iq.at[p], nk.at[p], ik.at[p], vec_s)
        for i, src in enumerate(early):
            if src is not None:
                leave(8 + 10 * p + i, src, per_pair[p][i])

    leave(38, w2_ref, w2_out)

    def attend(p, c):
        q, k, v = q_s[p], k_ref[p], v_ref[p]
        parts = []
        masked = [jnp.where(lane_head(rows, h)[0], q, BF16(0.0)) for h in range(2)]
        e = jnp.exp(dot_nt(jnp.concatenate(masked, axis=0), k)).astype(BF16)
        for h in range(2):
            mine, _ = lane_head(2 * rows, h)
            own_l, other = lane_head(rows, h)
            qm = masked[h]
            o = dot_nn(e[h * rows : h * rows + rows], jnp.where(mine, v, BF16(1.0)))
            parts.append(o / pltpu.roll(o, DH, 1))
            qx_ref[p, h] = jnp.where(own_l, qm, in_lanes(other, spread(-jnp.log(o))))
        own_l, _ = lane_head(rows, 0)
        out_ref[p] = jnp.where(own_l, parts[0], parts[1])
        return c

    lax.fori_loop(0, 3, attend, 0)
    for p in range(3):
        leave(8 + 10 * p + 1, qx_ref.at[p], per_pair[p][1])
        leave(8 + 10 * p + 4, out_ref.at[p], per_pair[p][4])
        attn_ref[:, 128 * p : 128 * p + 128] = out_ref[p].astype(BF16)
    arrive(own, tail, tail_out, sems.at[0])
    arrive(own, all_rows, q2_out, sems.at[1])
    arrive(own, all_rows, q13_out, sems.at[2])
    for copy in passed:
        copy.wait()


OUT_HEAD = (4, 3, 3)
FC1_HEAD = tuple((2 * QUARTER - ROW_FC1 - j + 11) // 12 for j in range(12))
FC2_HEAD = (3 * QUARTER - ROW_FC2) // 3


def mlp_kernel(
    t01, o_ref, cot0, cot1, tail_in, q2_in, q13_in, w2_in, c2_in,
    yk_ref, ys_ref, gmid_out, ga0, ga1_out, ga2_out, keep_ref, send_ref, wout_out,
    raw, quarters, slots, wo_s, w1_s, w2_s, x_s, act_s, n_s, hid_s, gb_s, db1_s, cot_s, sems, gmid_ref, ga1, ga2, wout_ref,
    q2_s, t01_s, attn_s, tail_s,
):
    own_len = cot0.shape[0]
    place = lax.axis_index("group")
    core = place % 2
    all_rows = pl.ds(0, PAD_Q)
    fetch(place, (q13_in, q13_in, c2_in, w2_in), all_rows, raw.at[0], sems.at[0])
    fetch(place, (c2_in, w2_in, q13_in, q13_in), all_rows, raw.at[1], sems.at[1])
    incoming = [
        pltpu.make_async_copy(src, dst, sems.at[6 + i])
        for i, (src, dst) in enumerate((
            (q2_in, q2_s), (t01, t01_s), (o_ref, attn_s), (tail_in, tail_s),
            (cot0, cot_s.at[pl.ds(0, own_len)]), (cot1, cot_s.at[pl.ds(own_len, own_len)]),
        ))
    ]
    for copy in incoming:
        copy.start()
    for copy in incoming:
        copy.wait()
    x_s[...] = t01_s[...].astype(F32)
    attn = attn_s[...]
    quarters[1] = q2_s[...].astype(F32)
    for i in range(2):
        arrive(q2_in, all_rows, raw.at[i], sems.at[i])
        quarters[2 * i] = raw[i].astype(F32)
    first = tail_s[...].astype(F32)
    vec = quarters[2, VEC_AT : VEC_AT + 40, :]
    bias_out, gain_two, bias_two = row_of(vec, 16, 3), row_of(vec, 19, 3), row_of(vec, 22, 3)
    bias_fc1, bias_fc2 = row_of(vec, 25, 12), row_of(vec, 37, 3)
    q1, q2, q3 = quarters.at[0], quarters.at[1], quarters.at[2]
    for j in range(3):
        n = OUT_HEAD[j]
        top = jnp.concatenate([first[3 * i + j : 3 * i + j + 1] for i in range(n)], axis=0)
        rest = q1[pl.ds(3 * n + j - 10, D - n, stride=3), :]
        wo_s[:, 128 * j : 128 * j + 128] = jnp.concatenate([top, rest], axis=0).astype(BF16)
        top = q2[pl.ds(ROW_FC2 - 2 * QUARTER + j, FC2_HEAD, stride=3), :]
        rest = q3[pl.ds(j, FF - FC2_HEAD, stride=3), :]
        w2_s[:, 128 * j : 128 * j + 128] = jnp.concatenate([top, rest], axis=0).astype(BF16)
    for j in range(12):
        n = FC1_HEAD[j]
        top = q1[pl.ds(ROW_FC1 - QUARTER + j, n, stride=12), :]
        rest = q2[pl.ds(ROW_FC1 - 2 * QUARTER + 12 * n + j, D - n, stride=12), :]
        w1_s[:, 128 * j : 128 * j + 128] = jnp.concatenate([top, rest], axis=0).astype(BF16)

    mid = x_s[...] + dot_nn(attn, wo_s[...]) + bias_out
    n, inv = norm(mid)
    n_s[...] = n
    act_s[...] = (n * gain_two + bias_two).astype(BF16)
    width = 256
    for at in range(0, FF, width):
        x = dot_nn(act_s[...], w1_s[:, at : at + width]) + bias_fc1[:, at : at + width]
        phi = 0.5 * (1.0 + lax.erf(x * INV_ROOT_TWO))
        hid_s[:, at : at + width] = (x * phi).astype(BF16)
        slope = phi + x * jnp.exp(-0.5 * x * x) * INV_ROOT_TAU
        gb = (dot_nt(cot_s[...], w2_s[at : at + width, :]) * slope).astype(BF16)
        gb_s[:, at : at + width] = gb
        db1_s[:, at : at + width] = jnp.sum(gb.astype(F32), 0, keepdims=True)
    hid, gb = hid_s[...], gb_s[...]
    y = mid + bias_fc2 + dot_nn(hid, w2_s[...])
    dw2 = dot_tn(hid, cot_s[...])
    for j in range(3):
        piece = dw2[:, 128 * j : 128 * j + 128]
        slots[pl.ds(SLOT + ROW_FC2 - 2 * QUARTER + j, FC2_HEAD, stride=3), :] = piece[:FC2_HEAD]
        slots[pl.ds(2 * SLOT + j, FF - FC2_HEAD, stride=3), :] = piece[FC2_HEAD:]
    dw1 = dot_tn(act_s[...], gb)
    for j in range(12):
        n1 = FC1_HEAD[j]
        piece = dw1[:, 128 * j : 128 * j + 128]
        slots[pl.ds(ROW_FC1 - QUARTER + j, n1, stride=12), :] = piece[:n1]
        slots[pl.ds(SLOT + ROW_FC1 - 2 * QUARTER + 12 * n1 + j, D - n1, stride=12), :] = piece[n1:]
    yk_ref[...] = y[0:own_len, :].astype(BF16)
    ys_ref[...] = y[own_len:, :].astype(BF16)
    gn = dot_nt(gb, w1_s[...])
    cot = cot_s[...].astype(F32)
    gmid = cot + norm_back(gn * gain_two, n_s[...], inv)
    gmid_ref[...] = gmid
    gproj = gmid.astype(BF16)
    gattn = dot_nt(gproj, wo_s[...]).astype(BF16)
    for p, ref in enumerate((ga0, ga1, ga2)):
        ref[...] = gattn[:, 128 * p : 128 * p + 128]
    leaving = [
        pltpu.make_async_copy(src, dst, sems.at[2 + i])
        for i, (src, dst) in enumerate(((gmid_ref, gmid_out), (ga1, ga1_out), (ga2, ga2_out), (wout_ref, wout_out)))
    ]
    for copy in leaving[:3]:
        copy.start()
    dwo = dot_tn(attn, gproj)
    for j in range(3):
        n0 = OUT_HEAD[j]
        piece = dwo[:, 128 * j : 128 * j + 128]
        slots[pl.ds(QUARTER + j, n0, stride=3), :] = piece[:n0]
        slots[pl.ds(3 * n0 + j - 10, D - n0, stride=3), :] = piece[n0:]
    slots[QUARTER + 10 : SLOT, :] = jnp.zeros((SLOT - QUARTER - 10, 128), F32)
    slots[SLOT + QUARTER : 2 * SLOT, :] = jnp.zeros((SLOT - QUARTER, 128), F32)
    slots[2 * SLOT + VEC_AT : 3 * SLOT, :] = jnp.zeros((SLOT - VEC_AT, 128), F32)

    def put(at, row):
        for i in range(row.shape[1] // 128):
            slots[2 * SLOT + VEC_AT + at + i : 2 * SLOT + VEC_AT + at + i + 1, :] = row[:, 128 * i : 128 * i + 128]

    put(16, jnp.sum(gproj.astype(F32), 0, keepdims=True))
    put(19, jnp.sum(gn * n_s[...], 0, keepdims=True))
    put(22, jnp.sum(gn, 0, keepdims=True))
    put(25, db1_s[...])
    put(37, jnp.sum(cot, 0, keepdims=True))
    wout_ref[0:10, :] = slots[QUARTER : QUARTER + 10, :].astype(BF16)
    wout_ref[10:, :] = jnp.zeros((54, 128), BF16)
    leaving[3].start()

    def deal(odd, even):
        for i in range(2):
            odd[i * SLOT : i * SLOT + SLOT, :] = slots[2 * i * SLOT : 2 * i * SLOT + SLOT, :].astype(BF16)
            at = SLOT + i * HALF
            even[i * SLOT : i * SLOT + HALF, :] = slots[at : at + HALF, :].astype(BF16)
            even[i * SLOT + HALF : i * SLOT + SLOT, :] = jnp.zeros((HALF, 128), BF16)

    @pl.when(core == 0)
    def _():
        deal(send_ref, keep_ref)

    @pl.when(core != 0)
    def _():
        deal(keep_ref, send_ref)

    for copy in leaving:
        copy.wait()


def pairs_back_kernel(*refs, pair):
    ins, ga_ref, refs = refs[:10], refs[10], refs[11:]
    bufs, in_sems = refs[-11:-1], refs[-1]
    refs = refs[:-11]
    incoming = [pltpu.make_async_copy(src, dst, in_sems.at[i]) for i, (src, dst) in enumerate(zip(ins, bufs))]
    for i in (9, 2, 1, 4, 3, 5, 6, 7, 8, 0):
        incoming[i].start()
    act_ref, qx_ref, k_ref, v_ref, out_ref, nq_ref, iq_ref, nk_ref, ik_ref, vec_ref = bufs
    if pair == 0:
        keep_in, send_in, g_out, sums_ref, keep_any, send_any, part, sems, g_ref, g_sem = refs
    elif pair == 1:
        g_out, sums_ref, part, g_ref, g_sem = refs
    else:
        extra_in, (g_ref, sums_ref, go_ref, gt_ref, keep_ref, send_ref, part, vrow) = refs[:9], refs[9:17]
        extras = refs[17:26]
        tok_ref, w2_ref, gmid_ref, wout_ref, g0_ref, g1_ref, sums0, sums1, part1_ref = extras
        more = [
            pltpu.make_async_copy(src, dst, in_sems.at[10 + i]) for i, (src, dst) in enumerate(zip(extra_in, extras))
        ]
        for copy in more:
            copy.start()
    for i in (9, 2, 1, 4, 3):
        incoming[i].wait()
    core = lax.axis_index("group") % 2
    if pair == 0:
        moves = [
            pltpu.make_async_copy(src, dst, sems.at[i])
            for i, (src, dst) in enumerate(((keep_in, keep_any), (send_in, send_any)))
        ]
        for copy in moves:
            copy.start()
    rows = ga_ref.shape[0]
    gain_q, gain_k = pair_gains(vec_ref[...])
    matrix = head_mean_matrix()
    k, v, ga = k_ref[...], v_ref[...], ga_ref[...]
    inner = -float(DH) * head_mean(ga.astype(F32) * out_ref[...], matrix)
    terms = spread(pltpu.roll(inner, DH, 1))
    gq_t = jnp.zeros((128, rows), F32)
    gk = jnp.zeros((2 * rows, 128), F32)
    gv = jnp.zeros((2 * rows, 128), F32)
    for h in range(2):
        mine, other_all = lane_head(2 * rows, h)
        own, other = lane_head(rows, h)
        ones = jnp.where((other_all >= 0) & (other_all <= 2), 1.0, 0.0).astype(BF16)
        qx = qx_ref[h]
        gax = jnp.where(own, ga, in_lanes(other, terms))
        prob = jnp.exp(dot_nt(jnp.where(mine, k, ones), qx))
        gprob = dot_nt(jnp.where(mine, v, ones), gax)
        gs = (prob * gprob).astype(BF16)
        gv = gv + dot_nn(prob.astype(BF16), jnp.where(own, ga, BF16(0.0)))
        gk = gk + dot_nn(gs, jnp.where(own, qx, BF16(0.0)))
        gq_t = gq_t + dot_tn(jnp.where(mine, k, BF16(0.0)), gs)
    gq = (gq_t.T * SCALE).astype(BF16).astype(F32)
    gk = gk.astype(BF16).astype(F32)

    def head_back(u, n, inv, gain):
        dn = u * gain
        return (inv * (dn - head_mean(dn, matrix) - n * head_mean(dn * n, matrix))).astype(BF16)

    def total(a):
        return jnp.sum(a, 0, keepdims=True)

    for i in (5, 6, 7, 8, 0):
        incoming[i].wait()
    nq, nk = nq_ref[...].astype(F32), nk_ref[...].astype(F32)
    gq_b = head_back(gq, nq, iq_ref[...].astype(F32), gain_q)
    gk_b = head_back(gk, nk, ik_ref[...].astype(F32), gain_k)
    gv_b = gv.astype(BF16)
    g_ref[0:rows, 0:128] = gq_b
    g_ref[rows:, 0:128] = jnp.zeros((rows, 128), BF16)
    g_ref[:, 128:256] = gk_b
    g_ref[:, 256:384] = gv_b
    if pair < 2:
        g_copy = pltpu.make_async_copy(g_ref, g_out, g_sem)
        g_copy.start()
    sums_ref[0:1, :] = total(gq_b.astype(F32))
    sums_ref[1:2, :] = total(gk_b.astype(F32))
    sums_ref[2:3, :] = total(gv_b.astype(F32))
    sums_ref[3:4, :] = total(gq * nq)
    sums_ref[4:5, :] = total(gk * nk)
    sums_ref[5:8, :] = jnp.zeros((3, 128), F32)
    dwq = dot_tn(act_ref[0:rows, :], gq_b).astype(BF16)
    dwkv = dot_tn(act_ref[...], g_ref[:, 128:384]).astype(BF16)
    part[0:D, :] = dwq
    part[D : 2 * D, :] = dwkv[:, :128]
    part[2 * D : PAIR, :] = dwkv[:, 128:]
    if pair == 0:
        for copy in moves:
            copy.wait()

        def move(into):
            for h in range(2):
                at = h * SLOT + HALF
                into[at : at + EARLY_HALF, :] = part[h * EARLY_HALF : h * EARLY_HALF + EARLY_HALF, :]

        @pl.when(core == 0)
        def _():
            move(keep_any)

        @pl.when(core != 0)
        def _():
            move(send_any)
    if pair < 2:
        g_copy.wait()
        return
    for copy in more:
        copy.wait()
    own_len = rows // 2
    gain_one = row_of(vec_ref[...], 0, 3)
    d_gain = jnp.zeros((1, D), F32)
    d_bias = jnp.zeros((1, D), F32)
    for i in range(4):
        at = own_len * i
        cols = slice(0, D) if i < 2 else slice(128, D)
        u = sum(
            dot_nt(g[at : at + own_len, cols], w2_ref[p, :, cols])
            for p, g in enumerate((g0_ref, g1_ref, g_ref))
        )
        n, inv = norm(tok_ref[at : at + own_len, :].astype(F32))
        d_gain = d_gain + total(u * n)
        d_bias = d_bias + total(u)
        back = norm_back(u * gain_one, n, inv)
        if i < 2:
            go_ref[at : at + own_len, :] = gmid_ref[at : at + own_len, :] + back
        else:
            gt_ref[at - rows : at - rows + own_len, :] = back.astype(BF16)
    for i in range(3):
        vrow[i : i + 1, :] = d_gain[:, 128 * i : 128 * i + 128]
        vrow[3 + i : 4 + i, :] = d_bias[:, 128 * i : 128 * i + 128]
    sums = (sums0[...], sums1[...], sums_ref[...])
    for p, s in enumerate(sums):
        for t in range(3):
            vrow[6 + 3 * t + p : 7 + 3 * t + p, :] = s[t : t + 1, :]
    dgq = sums[0][3:4, :] + sums[1][3:4, :] + sums[2][3:4, :]
    dgk = sums[0][4:5, :] + sums[1][4:5, :] + sums[2][4:5, :]
    low, _ = lane_head(1, 0)
    vrow[15:16, :] = jnp.where(low, dgq + pltpu.roll(dgq, DH, 1), dgk + pltpu.roll(dgk, DH, 1))

    def deal(matrix_to, vector_to):
        matrix_to[0:PAIR, :] = part1_ref[...]
        matrix_to[PAIR : 2 * PAIR, :] = part[...]
        matrix_to[2 * PAIR :, :] = wout_ref[...]
        vector_to[...] = jnp.zeros((LATE, 128), BF16)
        vector_to[VEC_IN_LATE - 2 : VEC_IN_LATE + 30, :] = jnp.concatenate(
            [jnp.zeros((2, 128), F32), vrow[...], jnp.zeros((14, 128), F32)], axis=0
        ).astype(BF16)

    @pl.when(core == 0)
    def _():
        deal(keep_ref, send_ref)

    @pl.when(core != 0)
    def _():
        deal(send_ref, keep_ref)


def update_kernel(
    rate, decay, cat, got, weight, momentum, average,
    grad_out, momentum_out, average_out, weight_out, copy_out,
    full, slot, grad_s, momentum_s, average_s, weight_s, copy_s, sems, *, bits,
):
    collect(cat, got, full, slot, bits=bits)
    pieces = [slice(a, min(a + STEP, QUARTER)) for a in range(0, QUARTER, STEP)]
    copies = []

    def out(i, src, dst):
        copy = pltpu.make_async_copy(src, dst, sems.at[i])
        copy.start()
        copies.append(copy)

    for at in pieces:
        g = full[at, :]
        grad_s[at, :] = g
        momentum_s[at, :] = MOMENT * momentum[at, :] + g
    out(0, grad_s, grad_out)
    out(1, momentum_s, momentum_out)
    for at in pieces:
        w = weight[at, :] - rate[0] * (full[at, :] + MOMENT * momentum_s[at, :])
        weight_s[at, :] = w
        copy_s[at, :] = w.astype(BF16)
    out(2, weight_s, weight_out)
    out(3, copy_s, copy_out)
    for at in pieces:
        average_s[at, :] = decay[0] * average[at, :] + (1.0 - decay[0]) * weight_s[at, :]
    out(4, average_s, average_out)
    for copy in copies:
        copy.wait()


def collect(cat, got, out, slot, *, bits):
    place, rep = lax.axis_index("group"), lax.axis_index("replica")
    y = jnp.minimum(rep & bits[0], 1)
    t0, t1 = jnp.minimum(rep & bits[1], 1), jnp.minimum(rep & bits[-1], 1)
    t = jnp.where(place % 2 == 0, t0, t1)
    one, two = jnp.where(place % 2 == 0, 2, 1), jnp.where(place % 2 == 0, 1, 2)
    mine = 2 * y + t
    spots = (mine, mine ^ one, mine ^ two, 3 - mine)

    def blocks(into):
        for i in range(4):
            src = (cat, got)[i // 2]
            off = pl.multiple_of(spots[i] * BLOCK, 16)
            into[pl.ds(off, BLOCK), :] = src[(i % 2) * BLOCK : (i % 2) * BLOCK + BLOCK, :].astype(F32)

    @pl.when(place != 0)
    def _():
        blocks(out)

    @pl.when(place == 0)
    def _():
        blocks(slot)

        def rows(start, stop):
            late = start >= PAIR
            half, skip, base = (LATE_HALF, EARLY_HALF, PAIR) if late else (EARLY_HALF, 0, 0)
            pieces = []
            while start < stop:
                h = (start - base) // half
                end = min(stop, base + (h + 1) * half)
                row = h * HALF + skip + start - base - h * half
                pieces.append(slot[row : row + end - start, :])
                start = end
            return pieces[0] if len(pieces) == 1 else jnp.concatenate(pieces, axis=0)

        for p in range(3):
            for t in range(3):
                out[pl.ds(3 * t + p, D, stride=9), :] = rows(PAIR * p + D * t, PAIR * p + D * t + D)
        out[ROW_OUT : ROW_OUT + 10, :] = rows(3 * PAIR, 3 * PAIR + 10)


def shape(*dims, dtype=BF16):
    return jax.ShapeDtypeStruct(dims, dtype)


def vmem(*dims, dtype=BF16):
    return pltpu.VMEM(dims, dtype)


class Plan:
    def __init__(self, replicas):
        self.replicas = replicas
        self.bits = []
        while 2 ** len(self.bits) < replicas:
            self.bits.append(2 ** len(self.bits))
        self.thirds = (self.bits[1], self.bits[-1])
        self.rest = list(zip(self.bits[2:], self.bits[-2:0:-1]))

    def swap(self, a, dims, places=(0, 1, 2, 3)):
        pairs = []
        for rep in range(self.replicas):
            for place in places:
                dim = dims[place % 2]
                if dim is not None:
                    to = (rep, place ^ 2) if dim == "x" else (rep ^ dim, place)
                    pairs.append((place * self.replicas + rep, to[1] * self.replicas + to[0]))
        return lax.ppermute(a, ("group", "replica"), pairs)


FAR = pl.BlockSpec(memory_space=pltpu.HBM)
ON_CHIP = pl.BlockSpec(memory_space=pltpu.VMEM)
SCALAR = pl.BlockSpec(memory_space=pltpu.SMEM)


def call(kernel, args, outs, scratch=(), specs=None, out_specs=None, flops=0, aliases={}, mib=16):
    specs = [sp or ON_CHIP for sp in specs or [None] * len(args)]
    out_specs = [sp or ON_CHIP for sp in out_specs or [None] * len(outs)]
    spaces = {id(ON_CHIP): pltpu.VMEM, id(FAR): pltpu.HBM}
    args = [
        a if sp is SCALAR else pltpu.with_memory_space_constraint(a, spaces[id(sp)]) for a, sp in zip(args, specs)
    ]
    outs = tuple(spaces[id(sp)](o.shape, o.dtype) for o, sp in zip(outs, out_specs))
    return pl.pallas_call(
        kernel,
        out_shape=outs,
        in_specs=specs,
        out_specs=tuple(out_specs),
        scratch_shapes=list(scratch),
        cost_estimate=pl.CostEstimate(flops=flops, transcendentals=0, bytes_accessed=0) if flops else None,
        input_output_aliases=aliases,
        compiler_params=pltpu.CompilerParams(vmem_limit_bytes=mib << 20),
    )(*args)


def per_device(tokens, cotangent, weight, momentum, average, rate, step, replicas):
    _, own_len, _ = tokens.shape
    rows = 2 * own_len
    x, c = lax.axis_index("group") // 2, lax.axis_index("group") % 2
    plan = Plan(replicas)

    place, rep = lax.axis_index("group"), lax.axis_index("replica")
    y = jnp.minimum(rep & plan.bits[0], 1)
    t = jnp.minimum(rep & jnp.where(c == 0, plan.thirds[0], plan.thirds[1]), 1)
    at_1 = [b * SLOT for b in (jnp.where(c == 0, y, x), jnp.where(c == 0, 1 - y, 1 - x))]
    at_3 = [jnp.where(c == 0, b * LATE_HALF, 0) for b in (y, 1 - y)]
    at_4 = [b * HALF for b in (jnp.where(c == 0, 1 - x, y), jnp.where(c == 0, x, 1 - y))]
    at_5 = [b * BLOCK for b in (t, 1 - t)]

    def move(a, pairs):
        return lax.ppermute(a, "group", pairs)

    def beside_of(a):
        return move(a, [(0, 1), (1, 0), (2, 3), (3, 2)])

    def over_x(a):
        return move(a, [(0, 2), (1, 3), (2, 0), (3, 1)])

    def pick(a, i):
        return lax.dynamic_index_in_dim(a, i, 0, keepdims=False)

    t1 = over_x(pick(tokens, 1 - x))
    t0 = pick(tokens, x)
    own = jnp.pad(weight.reshape(QUARTER, 128).astype(BF16), ((0, PAD_Q - QUARTER), (0, 0)))
    tail = own[VEC_AT - 2 : VEC_AT + 46]
    vec_x = move(tail, [(1, 3), (3, 1)])
    w1 = move(own, [(0, 2), (2, 0)])
    beside = beside_of(own)
    w2 = move(own, [(1, 3), (3, 1)])
    cot0, cot1 = pick(cotangent, x), pick(cotangent, 1 - x)
    cot1 = over_x(cot1)
    vec_b = jnp.where(place == 1, vec_x, tail)
    vec_b = jnp.where(c == 1, vec_b, beside_of(vec_b))
    t23 = jnp.concatenate([beside_of(t0), beside_of(t1)])
    c1 = beside_of(w1)
    c2 = beside_of(w2)

    made = call(
        qkv_attend_kernel, (t0, t1, t23, vec_b, own, beside, w1, c1),
        (
            shape(3, D, D), shape(rows, D), shape(rows, D), shape(2 * rows, D),
            shape(PAD_Q, 128), shape(PAD_Q, 128), shape(16, 128),
        )
        + (
            shape(2 * rows, D), shape(2, rows, 128), shape(2 * rows, 128), shape(2 * rows, 128),
            shape(rows, 128, dtype=F32), shape(rows, 128), shape(rows, 128),
            shape(2 * rows, 128), shape(2 * rows, 128), shape(40, 128, dtype=F32),
        ) * 3,
        [
            vmem(ROW_OUT, 128), vmem(ROW_OUT, 128, dtype=F32), vmem(3, rows, 128),
            vmem(2 * rows, D), vmem(3, 2, rows, 128), vmem(3, 2 * rows, 128), vmem(3, 2 * rows, 128),
            vmem(3, rows, 128, dtype=F32), pltpu.SemaphoreType.DMA, pltpu.SemaphoreType.DMA((39,)),
            vmem(3, D, D), vmem(3, rows, 128), vmem(3, rows, 128), vmem(3, 2 * rows, 128), vmem(3, 2 * rows, 128),
            vmem(40, 128, dtype=F32),
        ],
        out_specs=[FAR, None] + [FAR] * 35, mib=20, flops=10 ** 10,
    )
    w_cols, attn, t01, tok_all, q2, q13, tail_rows = made[:7]
    yk, ys, gmid, ga0, ga1, ga2, keep, send, wout = call(
        mlp_kernel, (t01, attn, cot0, cot1, tail_rows, q2, q13, w2, c2),
        (
            shape(own_len, D), shape(own_len, D), shape(rows, D, dtype=F32),
            shape(rows, 128), shape(rows, 128), shape(rows, 128),
            shape(2 * SLOT, 128), shape(2 * SLOT, 128), shape(64, 128),
        ),
        [
            vmem(2, PAD_Q, 128), vmem(3, PAD_Q, 128, dtype=F32),
            vmem(3 * SLOT, 128, dtype=F32), vmem(D, D), vmem(D, FF), vmem(FF, D),
            vmem(rows, D, dtype=F32), vmem(rows, D), vmem(rows, D, dtype=F32),
            vmem(rows, FF), vmem(rows, FF), vmem(1, FF, dtype=F32), vmem(rows, D),
            pltpu.SemaphoreType.DMA((12,)), vmem(rows, D, dtype=F32), vmem(rows, 128), vmem(rows, 128), vmem(64, 128),
            vmem(PAD_Q, 128), vmem(rows, D), vmem(rows, D), vmem(16, 128),
        ],
        specs=[FAR] * 8 + [None], out_specs=[None, None, FAR, None, FAR, FAR, None, None, FAR], mib=30, flops=10 ** 10,
    )

    def add(a, b):
        return (a.astype(F32) + b.astype(F32)).astype(BF16)

    def split(at, rows, total):
        return tuple(total(lambda a: lax.dynamic_slice_in_dim(a, at[i], rows, 0)) for i in range(2))

    def tie(a, b):
        return lax.optimization_barrier((a, b))

    def back(pair, ga, extra=(), outs=(), scratch=()):
        ins = (made[7],) + tuple(made[8 + 10 * pair : 17 + 10 * pair])
        scratch = list(scratch)
        if pair < 2:
            scratch += [vmem(2 * rows, D), pltpu.SemaphoreType.DMA]
        else:
            scratch += [vmem(*a.shape, dtype=a.dtype) for a in extra]
        scratch += [vmem(*a.shape, dtype=a.dtype) for a in ins] + [pltpu.SemaphoreType.DMA((19,))]
        far = [FAR] * len(extra) if pair == 2 else [None] * len(extra)
        return call(
            lambda *refs: pairs_back_kernel(*refs, pair=pair), ins + (ga,) + tuple(extra),
            (shape(2 * rows, D), shape(8, 128, dtype=F32)) + tuple(outs), scratch,
            specs=[FAR] * 10 + [None] + far,
            out_specs=[FAR if pair < 2 else None] + [None] * (1 + len(outs)), flops=5 * 10 ** 9, mib=20,
        )

    got_y = over_x(ys)
    g0, s0, keep, send = back(
        0, ga0, (keep, send), (shape(2 * SLOT, 128), shape(2 * SLOT, 128)),
        [vmem(PAIR, 128), pltpu.SemaphoreType.DMA((2,))],
    )
    ga1, send = tie(ga1, send)
    arrived = beside_of(send)
    g1, s1, part1 = back(1, ga1, outs=(shape(PAIR, 128),))
    kept, sent = split(at_1, SLOT, lambda cut: add(cut(keep), cut(arrived)))
    part1, sent = tie(part1, sent)
    got = plan.swap(sent, (plan.bits[0], "x"))
    extra = (tok_all, w_cols, gmid, wout, g0, g1, s0, s1, part1)
    _, _, go, gt, keep_l, send_l = back(
        2, ga2, extra, (shape(rows, D, dtype=F32), shape(rows, D), shape(LATE, 128), shape(LATE, 128)),
        [vmem(PAIR, 128), vmem(16, 128, dtype=F32)],
    )
    arrived = beside_of(send_l)
    kept_l, sent = split(at_3, LATE_HALF, lambda cut: add(cut(keep_l), cut(arrived)))
    late = add(kept_l, plan.swap(sent, (plan.bits[0], "x")))
    late = jnp.where((c == 1) & (x == 0), BF16(0.0), late)

    def with_late(cut):
        below = jnp.where(c == 0, HALF + EARLY_HALF, SLOT - LATE_HALF)
        zeros = jnp.zeros((SLOT, 128), BF16)
        return add(add(cut(kept), cut(got)), cut(lax.dynamic_update_slice_in_dim(zeros, late, below, 0)))

    kept, sent = split(at_4, HALF, with_late)
    got = plan.swap(sent, ("x", plan.bits[0]))
    kept, sent = split(at_5, BLOCK, lambda cut: add(cut(kept), cut(got)))
    part = add(kept, plan.swap(sent, plan.thirds))
    for dims in plan.rest:
        part = add(part, plan.swap(part, dims))
    cat = jnp.concatenate([part, plan.swap(part, (plan.bits[0], plan.thirds[1]))])
    got = plan.swap(cat, (plan.thirds[0], plan.bits[0]))

    both = (go + beside_of(gt).astype(F32)).astype(BF16)
    got_g = over_x(both[own_len:])

    def given(kept, got):
        first = lax.broadcasted_iota(jnp.int32, tokens.shape, 0) == x
        return jnp.where(first, kept[None], got[None])

    out_tokens = given(yk, got_y)
    grad_tokens = given(both[:own_len], got_g)
    step_value = step.astype(F32)
    decay = jnp.minimum(DECAY_MAX, (1.0 + step_value) / (10.0 + step_value))
    as_rows = [a.reshape(QUARTER, 128) for a in (weight, momentum, average)]
    wide, narrow = shape(QUARTER, 128, dtype=F32), shape(QUARTER, 128)
    results = call(
        lambda *refs: update_kernel(*refs, bits=plan.bits), (rate, decay, cat, got, *as_rows),
        (wide,) * 4 + (narrow,),
        [vmem(SLOT, 128, dtype=F32)] * 2 + [vmem(QUARTER, 128, dtype=F32)] * 4
        + [vmem(QUARTER, 128), pltpu.SemaphoreType.DMA((5,))],
        mib=20, specs=[SCALAR] * 2 + [None] * 5, out_specs=[FAR] * 5,
    )
    return (out_tokens, grad_tokens) + tuple(a.reshape(-1) for a in results)


def solution(mesh):
    tok, flat = P("replica", "group", None), P("group")

    def body(*args):
        return per_device(*args, replicas=mesh.shape["replica"])

    return jax.shard_map(
        body,
        mesh=mesh,
        in_specs=(tok, tok, flat, flat, flat, P(), P()),
        out_specs=(tok, tok, flat, flat, flat, flat, flat),
        check_vma=False,
    )
```
